32 devices in a mesh: egrp: 2 (over x), space: 16 (over z, y, core).
Axes of the slice: x: 2, y: 2, z: 4, core: 2. Of those that a mesh axis runs over, the one named last changes fastest.
Arguments:
- dist: float32 [2, 1024, 64, 128], P(None, 'egrp', 'space'), may hold values from -12 to 12
- hist_x: bfloat16 [4, 2, 1024, 64, 128], P(None, None, 'egrp', 'space'), may hold values from -6 to 6
- hist_g: bfloat16 [4, 2, 1024, 64, 128], P(None, None, 'egrp', 'space'), may hold values from -12 to 12
- mobility: float32 [64, 128], P('space'), may hold values from 0.2 to 2
- region: int32 [64, 128], P('space'), may hold values from 0 to 3
- phonon_bins: int32 [4], replicated, may hold values from 48 to 64, as said below
- coupling: float32 [4], replicated, may hold values from 0.2 to 1.5
- hist_used: int32 [2, 4], replicated, may hold values 0 or 1
Outputs:
- drifted: float32 [2, 1024, 64, 128], P(None, 'egrp', 'space')
The draws below stay inside these ranges and needn't reach their ends.
Inputs may be any that keep to these rules, and one draw needn't show every extreme that they name: `phonon_bins`: each value lies in 48 to 64; both ends occur.
All inputs are finite; a program needn't handle non-finite values.
Results may differ from the reference program's by a relative error of at most 0.0003.
Values sent between devices are 32-bit elements; how exact they have to be, the bound alone decides.
A program may use at most 128 MiB of HBM per device.

```python
import math
import jax
import jax.numpy as jnp
from jax import lax

NE = 1024
HISTORY = 4
NREGION = 4
KMIN = 48
KMAX = 64
COLS = 64
NZC = 128
NROWS = 64


def draw_phonon_bins(key, part):
    values = jax.random.randint(key, (NREGION,), KMIN, KMAX + 1)
    first = jax.random.randint(jax.random.fold_in(key, 1), (), 0, NREGION)
    second = (first + 1 + jax.random.randint(jax.random.fold_in(key, 2), (), 0, NREGION - 1)) % NREGION
    values = values.at[first].set(KMAX)
    values = values.at[second].set(KMIN)
    return values.astype(jnp.int32)


def shared_field(key):
    shape = (2, NE, NROWS, NZC)
    energy_level = jnp.exp(jax.random.uniform(jax.random.fold_in(key, 11), (1, NE, 1, 1), jnp.float32, jnp.log(0.5), jnp.log(2.0)))
    row_level = jnp.exp(jax.random.uniform(jax.random.fold_in(key, 12), (1, 1, NROWS, 1), jnp.float32, jnp.log(0.5), jnp.log(2.0)))
    levels = energy_level * row_level
    base = jnp.clip(jax.random.normal(jax.random.fold_in(key, 13), shape, jnp.float32), -3.0, 3.0)
    return (levels, base)


def draw_dist(key, part):
    levels, base = shared_field(key)
    return jnp.clip(levels * base, -12.0, 12.0).astype(jnp.float32)


def draw_hist_g(key, part):
    levels, base = shared_field(key)
    shape = (HISTORY, 2, NE, NROWS, NZC)
    along = jnp.exp(jax.random.uniform(jax.random.fold_in(key, 3), (HISTORY, 1, 1, 1, 1), jnp.float32, jnp.log(0.2), jnp.log(0.8)))
    spread = jnp.exp(jax.random.uniform(jax.random.fold_in(key, 7), (HISTORY, 1, 1, 1, 1), jnp.float32, jnp.log(0.5), jnp.log(1.5)))
    noise = jnp.clip(jax.random.normal(jax.random.fold_in(key, 6), shape, jnp.float32), -3.0, 3.0)
    values = levels[None] * (spread * noise - along * base[None])
    return jnp.clip(values, -12.0, 12.0).astype(jnp.bfloat16)


def place_ends(values, key, least, top_value):
    longest = values.shape.index(max(values.shape))
    spots = []
    for shift in (0, 1):
        where = [jax.random.randint(jax.random.fold_in(key, axis), (), 0, length) for axis, length in enumerate(values.shape)]
        where[longest] = (where[longest] + shift) % values.shape[longest]
        spots.append(tuple(where))
    return values.at[spots[0]].set(least).at[spots[1]].set(top_value)


def level_of(rng, dims, shards, low, top_value):
    level, own = 1.0, jax.random.fold_in(rng, 6)
    for position, shards_of in shards:
        steps = jnp.exp(jax.random.uniform(jax.random.fold_in(own, position), (shards_of,), jnp.float32, low / len(shards), top_value / len(shards)))
        level = level * jnp.repeat(steps, dims[position] // shards_of).reshape([-1 if axis == position else 1 for axis in range(len(dims))])
    return level


def centred(key, shape, scale, bound, split=(), held_as=jnp.bfloat16):
    entries = jax.random.normal(key, shape, jnp.float32) * scale
    if len(split) > 0:
        entries = level_of(key, shape, split, -0.22, 0.18) * entries
    return jnp.clip(entries, min=-bound, max=bound).astype(held_as)


def setup_inputs(seed: int = 0) -> dict:
    splits = jax.random.split(jax.random.key(seed), 9)
    return {
        "dist": draw_dist(jax.random.fold_in(splits[8], 71), 0),
        "hist_x": centred(splits[1], (HISTORY, 2, NE, NROWS, NZC), 1.0, 6.0, ((2, 2), (3, 16))),
        "hist_g": draw_hist_g(jax.random.fold_in(splits[8], 71), 0),
        "mobility": jnp.clip(jnp.exp(math.log(2.0) - 2.3025851 * jax.random.uniform(splits[3], (NROWS, NZC), jnp.float32) ** level_of(splits[3], (NROWS, NZC), ((0, 16),), -0.2, 0.2)), 0.2, 2.0),
        "region": place_ends(jax.random.randint(splits[4], (NROWS, NZC), 0, NREGION), jax.random.fold_in(splits[4], 1), 0, NREGION - 1).astype(jnp.int32),
        "phonon_bins": draw_phonon_bins(jax.random.fold_in(splits[8], 71), 0),
        "coupling": jnp.clip(jnp.exp(jax.random.uniform(splits[6], (NREGION,), jnp.float32, math.log(0.2), math.log(1.5))), 0.2, 1.5),
        "hist_used": place_ends((jax.random.randint(splits[7], (2, HISTORY), 0, 2) < 1).astype(jnp.int32), jax.random.fold_in(splits[7], 1), 0, 1),
    }


def neighbour_sum(field, mobility):
    total = jnp.zeros(field.shape, jnp.float32)
    rows = field.shape[2]
    cells = field.shape[3]
    row_ids = jnp.arange(rows, dtype=jnp.int32)[:, None]
    cell_ids = jnp.arange(cells, dtype=jnp.int32)[None, :]
    column = cell_ids % COLS
    for shift_by, axis, valid in ((1, 0, row_ids > 0), (-1, 0, row_ids < rows - 1), (1, 1, column > 0), (-1, 1, column < COLS - 1), (COLS, 1, cell_ids >= COLS), (-COLS, 1, cell_ids < COLS)):
        moved = jnp.roll(field, shift_by, axis=axis + 2)
        moved_mob = jnp.roll(mobility, shift_by, axis=axis)
        flux = 0.5 * (mobility + moved_mob)
        total = total + jnp.where(valid, flux * (moved - field), 0.0)
    return total

def reference(dist, hist_x, hist_g, mobility, region, phonon_bins, coupling, hist_used):
    even = dist[0]
    odd = dist[1]
    energy_ids = jnp.arange(NE, dtype=jnp.int32)
    dos = jnp.sqrt((energy_ids.astype(jnp.float32) + 0.5) / NE)
    padded = jnp.pad(even, ((KMAX, KMAX), (0, 0), (0, 0)))
    shifted = jnp.zeros(even.shape, jnp.float32)
    outrate = jnp.zeros(even.shape, jnp.float32)
    lam = jnp.zeros(region.shape, jnp.float32)
    for index in range(NREGION):
        offset = phonon_bins[index].astype(jnp.int32)
        above = lax.dynamic_slice_in_dim(padded, (KMAX + offset).astype(jnp.int32), NE, 0)
        below = lax.dynamic_slice_in_dim(padded, (KMAX - offset).astype(jnp.int32), NE, 0)
        lower = energy_ids - offset
        upper = energy_ids + offset
        dos_low = jnp.where(lower >= 0, jnp.sqrt((jnp.maximum(lower, 0).astype(jnp.float32) + 0.5) / NE), 0.0)
        dos_high = jnp.where(upper < NE, jnp.sqrt((upper.astype(jnp.float32) + 0.5) / NE), 0.0)
        rate = coupling[index] * (1.5 * dos_low + 0.5 * dos_high)
        inside = (region == index)[None]
        shifted = jnp.where(inside, 1.5 * above + 0.5 * below, shifted)
        outrate = jnp.where(inside, rate[:, None, None], outrate)
        lam = jnp.where(region == index, coupling[index], lam)
    gain_in = lam[None] * dos[:, None, None] * shifted
    new_even = (even + gain_in) / (1.0 + outrate)
    new_odd = odd / (1.0 + outrate + lam[None])
    res = jnp.stack([new_even - even, new_odd - odd])
    fields = []
    for field in range(2):
        vectors = [res[field]] + [hist_g[index, field].astype(jnp.float32) for index in range(HISTORY)]
        gram = jnp.zeros((HISTORY + 1, HISTORY + 1), jnp.float32)
        for left in range(HISTORY + 1):
            for right in range(HISTORY + 1):
                gram = gram.at[left, right].set(jnp.sum(vectors[left] * vectors[right]))
        valid = jnp.concatenate([jnp.ones((1,), jnp.float32), hist_used[field].astype(jnp.float32)])
        masked = valid[:, None] * valid[None, :] * gram + jnp.diag(1.0 - valid) * gram[0, 0]
        factor = jnp.linalg.cholesky(masked)
        weights = jax.scipy.linalg.cho_solve((factor, True), valid)
        coeffs = weights / jnp.sum(weights)
        part_mix = coeffs[0] * (dist[field] + 0.5 * res[field])
        for index in range(HISTORY):
            part_mix = part_mix + coeffs[index + 1] * (hist_x[index, field].astype(jnp.float32) + 0.5 * hist_g[index, field].astype(jnp.float32))
        fields.append(part_mix)
    mixed = jnp.stack(fields)
    lap = neighbour_sum(mixed, mobility)
    drive = 0.25 * dos[:, None, None]
    out_even = mixed[0] + 0.08 * lap[0] + drive * mixed[1]
    out_odd = mixed[1] + 0.08 * lap[1] - drive * mixed[0]
    return jnp.stack([out_even, out_odd])
```

```python
import functools
import jax
import jax.numpy as jnp
from jax import lax
from jax.experimental import pallas as pl
from jax.experimental.pallas import tpu as pltpu
from jax.sharding import PartitionSpec as P

NE = 1024
HISTORY = 4
NREGION = 4
KMAX = 64
COLS = 64
PIECES = 8
EARLY = (2,)
HALO_PIECES = 4
STEP = 32
WIDE = 32
TABLE = 128 // NREGION
PAIRS = [(i, j) for i in range(HISTORY + 1) for j in range(i, HISTORY + 1)]
MESH = pl.DeviceIdType.MESH


def dos_of(energy):
    value = (energy.astype(jnp.float32) + 0.5) * (1.0 / NE)
    return value * lax.rsqrt(value)


def solve(total, field, used_ref):
    def entry(i, j):
        lane = field * len(PAIRS) + PAIRS.index((min(i, j), max(i, j)))
        return jnp.broadcast_to(total[:, lane : lane + 1], (8, 128))

    size = HISTORY + 1
    valid = [jnp.ones((8, 128), jnp.float32)]
    for index in range(HISTORY):
        valid.append(jnp.full((8, 128), used_ref[field, index].astype(jnp.float32)))
    first = entry(0, 0)
    low = [[None] * size for _ in range(size)]
    scaled = [[None] * size for _ in range(size)]
    inverse = [None] * size
    for j in range(size):
        for i in range(j, size):
            value = valid[i] * valid[j] * entry(i, j)
            if i == j:
                value = value + (1.0 - valid[i]) * first
            for k in range(j):
                value = value - scaled[i][k] * low[j][k]
            scaled[i][j] = value
        inverse[j] = 1.0 / scaled[j][j]
        for i in range(j + 1, size):
            low[i][j] = scaled[i][j] * inverse[j]
    forward = []
    for i in range(size):
        value = valid[i]
        for k in range(i):
            value = value - low[i][k] * forward[k]
        forward.append(value)
    weights = [None] * size
    for i in reversed(range(size)):
        value = forward[i] * inverse[i]
        for k in range(i + 1, size):
            value = value - low[k][i] * weights[k]
        weights[i] = value
    inv_sum = 1.0 / functools.reduce(lambda a, b: a + b, weights)
    return [w * inv_sum for w in weights]


def kernel(
    n_egrp, n_space, ne, rows,
    bins_hbm, coup_hbm, used_hbm, mob_hbm, region_hbm, dist_hbm, hx_hbm, hg_hbm,
    out,
    bins_ref, coup_ref, used_ref, mob_ref, region_ref,
    even, odd, hg, hx, base, hist, mixed, edges, packed, lo, hi, ahead, tables, tile, weight,
    mob_send, mob_lo, mob_hi, sums, part, gathered, halo,
    in_sem, small_sem, halo_send, halo_recv, mob_ssem, mob_rsem, sum_send, sum_recv,
    edge_send, edge_recv, ahead_send, ahead_recv,
):
    my_e = lax.axis_index("egrp")
    my_s = lax.axis_index("space")
    count = n_egrp * n_space
    me = my_e * n_space + my_s
    total_rows = ne * rows
    pad = KMAX * rows
    group = 8 // rows
    piece = ne // PIECES
    spans = [pl.ds(index * piece, piece) for index in range(PIECES)]
    late_pieces = [index for index in range(PIECES) if index not in EARLY]

    def device(index):
        return (index // n_space, lax.rem(index, n_space))

    small = [
        pltpu.make_async_copy(source, target, small_sem.at[index])
        for index, (source, target) in enumerate((
            (region_hbm, region_ref), (bins_hbm, bins_ref), (coup_hbm, coup_ref),
            (mob_hbm, mob_ref), (used_hbm, used_ref),
        ))
    ]
    first_early, last_early = EARLY[0], EARLY[-1] + 1
    cuts = [0, first_early * piece * rows, last_early * piece * rows, total_rows]
    parts = [pl.ds(cuts[index], cuts[index + 1] - cuts[index]) for index in range(3)]

    def history_load(source, target, index, sem):
        return pltpu.make_async_copy(
            source.at[:, :, parts[index]], target.at[:, :, parts[index]], in_sem.at[sem]
        )

    first = [history_load(hx_hbm, hx, 1, 2), history_load(hg_hbm, hg, 1, 3)]
    loads = [
        pltpu.make_async_copy(dist_hbm.at[0], even.at[pl.ds(pad, total_rows)], in_sem.at[0]),
        pltpu.make_async_copy(dist_hbm.at[1], odd, in_sem.at[1]),
        history_load(hg_hbm, hg, 2, 4),
        history_load(hg_hbm, hg, 0, 5),
    ]
    late = [history_load(hx_hbm, hx, 0, 6), history_load(hx_hbm, hx, 2, 7)]
    for copy in small + first + loads + late:
        copy.start()

    barrier = pltpu.get_barrier_semaphore()

    def greet(step, carry):
        pl.semaphore_signal(
            barrier, inc=1, device_id=device(lax.rem(me + step, count)), device_id_type=MESH
        )
        return carry

    lax.fori_loop(n_space, count, greet, 0)
    lax.fori_loop(1, n_space, greet, 0)

    has_below_e = my_e > 0
    has_above_e = my_e < n_egrp - 1
    has_below = my_s > 0
    has_above = my_s < n_space - 1

    for copy in small:
        copy.wait()
    for copy_of in range(group):
        tile[pl.ds(copy_of * rows, rows), :] = region_ref[...]
    mob_send[0] = mob_ref[0:1, :]
    mob_send[1] = mob_ref[rows - 1 : rows, :]

    for field in range(2):
        mixed[field, pl.ds(0, 8), :] = jnp.zeros((8, 128), jnp.float32)
        mixed[field, pl.ds(8 + total_rows, 8), :] = jnp.zeros((8, 128), jnp.float32)

    even[pl.ds(0, pad), :] = jnp.zeros((pad, 128), jnp.float32)
    even[pl.ds(pad + total_rows, pad), :] = jnp.zeros((pad, 128), jnp.float32)

    @pl.when(my_s == 0)
    def _():
        lo[...] = jnp.zeros(lo.shape, jnp.float32)
        ahead[0] = jnp.zeros(ahead.shape[1:], jnp.float32)
        mob_lo[...] = jnp.zeros(mob_lo.shape, jnp.float32)

    @pl.when(my_s == n_space - 1)
    def _():
        hi[...] = jnp.zeros(hi.shape, jnp.float32)
        ahead[1] = jnp.zeros(ahead.shape[1:], jnp.float32)
        mob_hi[...] = jnp.zeros(mob_hi.shape, jnp.float32)

    pl.semaphore_wait(barrier, count - 1)

    chunk = pad // HALO_PIECES
    halos = []
    for index in range(HALO_PIECES):
        up_e = pltpu.make_async_remote_copy(
            dist_hbm.at[0, pl.ds(total_rows - pad + index * chunk, chunk)],
            halo.at[0, index],
            halo_send.at[0, index], halo_recv.at[0, index],
            device_id=(lax.rem(my_e + 1, n_egrp), my_s), device_id_type=MESH,
        )
        down_e = pltpu.make_async_remote_copy(
            dist_hbm.at[0, pl.ds(index * chunk, chunk)],
            halo.at[1, index],
            halo_send.at[1, index], halo_recv.at[1, index],
            device_id=(lax.rem(my_e + n_egrp - 1, n_egrp), my_s), device_id_type=MESH,
        )
        halos.append((up_e, down_e))
    next_s = lax.rem(my_s + 1, n_space)
    prev_s = lax.rem(my_s + n_space - 1, n_space)

    def pair(up_source, up_target, down_source, down_target, send, recv):
        return (
            pltpu.make_async_remote_copy(
                up_source, up_target, send[0], recv[0],
                device_id=(my_e, next_s), device_id_type=MESH,
            ),
            pltpu.make_async_remote_copy(
                down_source, down_target, send[1], recv[1],
                device_id=(my_e, prev_s), device_id_type=MESH,
            ),
        )

    def start(copies):
        @pl.when(has_above)
        def _():
            copies[0].start()

        @pl.when(has_below)
        def _():
            copies[1].start()

    def arrive(copies):
        @pl.when(has_below)
        def _():
            copies[0].wait_recv()

        @pl.when(has_above)
        def _():
            copies[1].wait_recv()

    mobs = pair(
        mob_send.at[1], mob_lo, mob_send.at[0], mob_hi,
        [mob_ssem.at[0], mob_ssem.at[1]], [mob_rsem.at[0], mob_rsem.at[1]],
    )

    @pl.when(has_above_e)
    def _():
        for up_e, _ in halos:
            up_e.start()

    @pl.when(has_below_e)
    def _():
        for _, down_e in halos:
            down_e.start()

    start(mobs)

    def join_history(step, carry):
        row = pl.multiple_of(step * STEP, STEP)
        for index in range(HISTORY):
            for field in range(2):
                hist[index, field, pl.ds(row, STEP), :] = hx[
                    index, field, pl.ds(row, STEP), :
                ].astype(jnp.float32) + 0.5 * hg[index, field, pl.ds(row, STEP), :].astype(
                    jnp.float32
                )
        return carry

    def pack(terms, step, carry):
        start_at = pl.multiple_of(step * 8, 8)
        for field in range(2):
            for side, row in ((0, 0), (1, rows - 1)):
                for term in terms:
                    at = pl.ds(start_at * rows + row, 8, stride=rows)
                    value = base[field, at, :] if term == 0 else hist[term - 1, field, at, :]
                    edges[side, term, field, pl.ds(start_at, 8), :] = value
        return carry

    pack_base = functools.partial(pack, (0,))
    pack_hist = functools.partial(pack, tuple(range(1, HISTORY + 1)))
    pack_all = functools.partial(pack, tuple(range(HISTORY + 1)))
    per_piece = piece * rows // STEP

    for copy in first:
        copy.wait()
    early_sends = []
    for place, index in enumerate(EARLY):
        lax.fori_loop(index * per_piece, (index + 1) * per_piece, join_history, 0)
        lax.fori_loop(index * (piece // 8), (index + 1) * (piece // 8), pack_hist, 0)
        terms = pl.ds(1, HISTORY)
        here = pl.ds(place * piece, piece)
        copies = pair(
            edges.at[1, terms, :, spans[index]], ahead.at[0, terms, :, here],
            edges.at[0, terms, :, spans[index]], ahead.at[1, terms, :, here],
            [ahead_send.at[side, 0, place] for side in range(2)],
            [ahead_recv.at[side, 0, place] for side in range(2)],
        )
        start(copies)
        early_sends.append(copies)

    lanes = lax.broadcasted_iota(jnp.int32, (8, 128), 1)
    sublanes = lax.broadcasted_iota(jnp.int32, (8, 128), 0)
    which = lanes % NREGION
    bins = jnp.zeros((8, 128), jnp.int32)
    lam = jnp.zeros((8, 128), jnp.float32)
    for index in range(NREGION):
        bins = jnp.where(which == index, bins_ref[index], bins)
        lam = jnp.where(which == index, coup_ref[index], lam)
    within = (lanes // NREGION) * group + sublanes // rows

    def fill_tables(step, carry):
        energy = my_e * ne + step * (TABLE * group) + within
        lower = energy - bins
        upper = energy + bins
        dos_low = jnp.where(lower >= 0, dos_of(jnp.maximum(lower, 0)), 0.0)
        dos_high = jnp.where(upper < NE, dos_of(upper), 0.0)
        rate = lam * (1.5 * dos_low + 0.5 * dos_high)
        inverse = 1.0 / (1.0 + rate)
        tables[step, 0] = -rate * inverse
        tables[step, 1] = 0.5 * lam * dos_of(energy) * inverse
        tables[step, 2] = -(rate + lam) / (1.0 + rate + lam)
        return carry

    lax.fori_loop(0, total_rows // (8 * TABLE), fill_tables, 0)

    for copy in loads:
        copy.wait()

    subs = STEP // 8
    per_table = TABLE // subs

    def residuals(step, accs):
        row = pl.multiple_of(step * STEP, STEP)
        region = tile[...]
        chosen = [region == index for index in range(1, NREGION)]
        scale = [[], [], []]
        table_at = step // per_table
        offset = lax.rem(step, per_table) * subs
        for sub in range(subs):
            lane = region + (offset + sub) * NREGION
            for kind in range(3):
                scale[kind].append(
                    jnp.take_along_axis(
                        tables[table_at, kind], lane, axis=1, mode="promise_in_bounds"
                    )
                )
        above, below = [], []
        for index in range(NREGION):
            shift = bins_ref[index] * rows
            up = even[pl.ds(pad + row + shift, STEP), :]
            down = even[pl.ds(pad + row - shift, STEP), :]
            for sub in range(subs):
                at = slice(sub * 8, sub * 8 + 8)
                if index == 0:
                    above.append(up[at])
                    below.append(down[at])
                else:
                    above[sub] = jnp.where(chosen[index - 1], up[at], above[sub])
                    below[sub] = jnp.where(chosen[index - 1], down[at], below[sub])
        own_even = even[pl.ds(pad + row, STEP), :]
        own_odd = odd[pl.ds(row, STEP), :]
        res = [[], []]
        for sub in range(subs):
            at = slice(sub * 8, sub * 8 + 8)
            res[0].append(
                scale[0][sub] * own_even[at] + scale[1][sub] * (3.0 * above[sub] + below[sub])
            )
            res[1].append(scale[2][sub] * own_odd[at])
            base[0, pl.ds(row + sub * 8, 8), :] = own_even[at] + 0.5 * res[0][sub]
            base[1, pl.ds(row + sub * 8, 8), :] = own_odd[at] + 0.5 * res[1][sub]
        new = []
        for field in range(2):
            older = [
                hg[index, field, pl.ds(row, STEP), :].astype(jnp.float32)
                for index in range(HISTORY)
            ]
            vectors = [res[field]] + [
                [value[sub * 8 : sub * 8 + 8] for sub in range(subs)] for value in older
            ]
            for position, (i, j) in enumerate(PAIRS):
                value = accs[field * len(PAIRS) + position]
                for sub in range(subs):
                    value = value + vectors[i][sub] * vectors[j][sub]
                new.append(value)
        return tuple(new)

    accs = tuple(jnp.zeros((8, 128), jnp.float32) for _ in range(2 * len(PAIRS)))
    edge = pad // STEP
    steps = total_rows // STEP
    first_free = jnp.where(has_below_e, edge, 0)
    last_free = jnp.where(has_above_e, steps - edge, steps)
    accs = lax.fori_loop(first_free, last_free, residuals, accs)

    reach = edge // HALO_PIECES
    for index in range(HALO_PIECES):
        @pl.when(has_below_e)
        def _():
            halos[index][0].wait_recv()
            even[pl.ds(index * chunk, chunk), :] = halo[0, index]

        if index == 0:
            continue
        stop = edge if index == HALO_PIECES - 1 else index * reach
        accs = lax.fori_loop(
            jnp.where(has_below_e, (index - 1) * reach, 0),
            jnp.where(has_below_e, stop, 0), residuals, accs,
        )
    for index in range(HALO_PIECES):
        @pl.when(has_above_e)
        def _():
            halos[index][1].wait_recv()
            even[pl.ds(pad + total_rows + index * chunk, chunk), :] = halo[1, index]

        accs = lax.fori_loop(
            jnp.where(has_above_e, steps - edge + index * reach, steps),
            jnp.where(has_above_e, steps - edge + (index + 1) * reach, steps), residuals, accs,
        )

    sums[...] = jnp.zeros(sums.shape, jnp.float32)
    for position, acc in enumerate(accs):
        sums[position : position + 1, :] = jnp.sum(acc, axis=0, keepdims=True)
    lane_sum = jnp.sum(sums[...], axis=1, keepdims=True)
    place = lax.broadcasted_iota(jnp.int32, sums.shape, 0) == lax.broadcasted_iota(
        jnp.int32, sums.shape, 1
    )
    row_sum = jnp.sum(jnp.where(place, lane_sum, 0.0), axis=0, keepdims=True)
    part[...] = row_sum
    gathered[me] = row_sum

    def send_sums(step, carry):
        pltpu.make_async_remote_copy(
            part, gathered.at[me], sum_send, sum_recv,
            device_id=device(lax.rem(me + step, count)), device_id_type=MESH,
        ).start()
        return carry

    lax.fori_loop(1, count, send_sums, 0)

    for place, index in enumerate(EARLY):
        lax.fori_loop(index * (piece // 8), (index + 1) * (piece // 8), pack_base, 0)
        here = pl.ds(place * piece, piece)
        copies = pair(
            edges.at[1, 0, :, spans[index]], ahead.at[0, 0, :, here],
            edges.at[0, 0, :, spans[index]], ahead.at[1, 0, :, here],
            [ahead_send.at[side, 1, place] for side in range(2)],
            [ahead_recv.at[side, 1, place] for side in range(2)],
        )
        start(copies)
        early_sends.append(copies)

    for copy in late:
        copy.wait()
    lax.fori_loop(0, first_early * per_piece, join_history, 0)
    lax.fori_loop(last_early * per_piece, steps, join_history, 0)
    lax.fori_loop(0, first_early * (piece // 8), pack_all, 0)
    lax.fori_loop(last_early * (piece // 8), ne // 8, pack_all, 0)

    arrive(mobs)

    lanes = lax.broadcasted_iota(jnp.int32, (1, 128), 1)
    column = lanes % COLS
    none = jnp.zeros((1, 128), jnp.float32)
    for row in range(rows):
        mob = mob_ref[row : row + 1, :]
        under = mob_lo[...] if row == 0 else mob_ref[row - 1 : row, :]
        over = mob_hi[...] if row == rows - 1 else mob_ref[row + 1 : row + 2, :]
        w_under = 0.04 * (mob + under)
        w_over = 0.04 * (mob + over)
        if row == 0:
            w_under = jnp.where(has_below, w_under, 0.0)
        if row == rows - 1:
            w_over = jnp.where(has_above, w_over, 0.0)
        w_left = jnp.where(column > 0, 0.04 * (mob + pltpu.roll(mob, 1, 1)), 0.0)
        w_right = jnp.where(column < COLS - 1, 0.04 * (mob + pltpu.roll(mob, 127, 1)), 0.0)
        w_plane = 0.04 * (mob + pltpu.roll(mob, COLS, 1))
        own = 1.0 - (w_under + w_over + w_left + w_right + w_plane)
        rows_of = (
            own,
            none if row == 0 else w_under,
            none if row == rows - 1 else w_over,
            w_left,
            w_right,
            w_plane,
            w_under if row == 0 else w_over if row == rows - 1 else none,
        )
        for place, value in enumerate(rows_of):
            for copy_of in range(group):
                weight[place, copy_of * rows + row : copy_of * rows + row + 1, :] = value

    sums_in = gathered.at[pl.ds(0, count - 1)]
    pltpu.make_async_copy(sums_in, sums_in, sum_recv).wait()
    total = jnp.sum(gathered[...], axis=0)
    narrow = [solve(total, field, used_ref) for field in range(2)]

    def mix_edges(step, carry):
        at = pl.ds(pl.multiple_of(step * 8, 8), 8)
        for field in range(2):
            for side in range(2):
                value = narrow[field][0] * edges[side, 0, field, at, :]
                for index in range(1, HISTORY + 1):
                    value = value + narrow[field][index] * edges[side, index, field, at, :]
                packed[side, field, at, :] = value
        return carry

    sends = {}
    for index in late_pieces:
        lax.fori_loop(index * (piece // 8), (index + 1) * (piece // 8), mix_edges, 0)
        copies = pair(
            packed.at[1, :, spans[index]], lo.at[:, spans[index]],
            packed.at[0, :, spans[index]], hi.at[:, spans[index]],
            [edge_send.at[side, index] for side in range(2)],
            [edge_recv.at[side, index] for side in range(2)],
        )
        start(copies)
        sends[index] = copies

    coeffs = [
        [jnp.concatenate([c] * (WIDE // 8), axis=0) for c in narrow[field]] for field in range(2)
    ]
    blocks = piece * rows // WIDE

    def mix(block, carry):
        row = pl.multiple_of(block * WIDE, WIDE)
        for field in range(2):
            value = coeffs[field][0] * base[field, pl.ds(row, WIDE), :]
            for index in range(HISTORY):
                value = value + coeffs[field][index + 1] * hist[index, field, pl.ds(row, WIDE), :]
            mixed[field, pl.ds(8 + row, WIDE), :] = value
        return carry

    lax.fori_loop(0, PIECES * blocks, mix, 0)

    weights = [weight[place] for place in range(7)]

    def drift(block, carry):
        for part_of in range(WIDE // 8):
            row = pl.multiple_of(block * WIDE + part_of * 8, 8)
            energy = my_e * ne + (row + lax.broadcasted_iota(jnp.int32, (8, 128), 0)) // rows
            drive = 0.25 * dos_of(energy)
            own = [mixed[field, pl.ds(8 + row, 8), :] for field in range(2)]
            for field in range(2):
                value = own[field]
                result = (
                    weights[0] * value
                    + weights[1] * mixed[field, pl.ds(7 + row, 8), :]
                    + weights[2] * mixed[field, pl.ds(9 + row, 8), :]
                    + weights[3] * pltpu.roll(value, 1, 1)
                    + weights[4] * pltpu.roll(value, 127, 1)
                    + weights[5] * pltpu.roll(value, COLS, 1)
                )
                if field == 0:
                    result = result + drive * own[1]
                else:
                    result = result - drive * own[0]
                out[field, pl.ds(row, 8), :] = result
        return carry

    lax.fori_loop(0, PIECES * blocks, drift, 0)

    sublane = lax.broadcasted_iota(jnp.int32, (8, 128), 0)
    places = [
        (sublane < (copy_of * rows + rows // 2), sublane < (copy_of + 1) * rows)
        for copy_of in range(group)
    ]

    def add_edges(block, carry):
        for part_of in range(WIDE // 8):
            row = pl.multiple_of(block * WIDE + part_of * 8, 8)
            first = block * (WIDE // rows) + part_of * group
            for field in range(2):
                value = None
                for copy_of in reversed(range(group)):
                    from_hi = hi[field, pl.ds(first + copy_of, 8, stride=0), :]
                    from_lo = lo[field, pl.ds(first + copy_of, 8, stride=0), :]
                    if value is None:
                        value = from_hi
                    else:
                        value = jnp.where(places[copy_of][1], from_hi, value)
                    value = jnp.where(places[copy_of][0], from_lo, value)
                out[field, pl.ds(row, 8), :] = out[field, pl.ds(row, 8), :] + weights[6] * value
        return carry

    for copies in early_sends:
        arrive(copies)
    for place, index in enumerate(EARLY):

        def mix_early(step, carry):
            at = pl.ds(pl.multiple_of(place * piece + step * 8, 8), 8)
            to = pl.ds(pl.multiple_of(index * piece + step * 8, 8), 8)
            for side, target in ((0, lo), (1, hi)):
                for field in range(2):
                    value = narrow[field][0] * ahead[side, 0, field, at, :]
                    for term in range(1, HISTORY + 1):
                        value = value + narrow[field][term] * ahead[side, term, field, at, :]
                    target[field, to, :] = value
            return carry

        lax.fori_loop(0, piece // 8, mix_early, 0)
        lax.fori_loop(index * blocks, (index + 1) * blocks, add_edges, 0)

    for index in late_pieces:
        arrive(sends[index])
        lax.fori_loop(index * blocks, (index + 1) * blocks, add_edges, 0)

    sums_out = gathered.at[pl.ds(0, count - 1)]
    pltpu.make_async_copy(sums_out, sums_out, sum_send).wait()

    @pl.when(has_above_e)
    def _():
        for up_e, _ in halos:
            up_e.wait_send()

    @pl.when(has_below_e)
    def _():
        for _, down_e in halos:
            down_e.wait_send()

    sent = [mobs] + early_sends + list(sends.values())

    @pl.when(has_above)
    def _():
        for up, _ in sent:
            up.wait_send()

    @pl.when(has_below)
    def _():
        for _, down in sent:
            down.wait_send()


def local(n_egrp, n_space, dist, hist_x, hist_g, mobility, region, phonon_bins, coupling, hist_used):
    ne, rows = dist.shape[1], dist.shape[2]
    total = ne * rows
    pad = KMAX * rows
    count = n_egrp * n_space
    f32 = jnp.float32
    vmem = pl.BlockSpec(memory_space=pltpu.VMEM)
    hbm = pl.BlockSpec(memory_space=pltpu.HBM)
    result = pl.pallas_call(
        functools.partial(kernel, n_egrp, n_space, ne, rows),
        out_shape=jax.ShapeDtypeStruct((2, total, 128), f32),
        in_specs=[hbm] * 8,
        out_specs=vmem,
        scratch_shapes=[
            pltpu.SMEM((NREGION,), jnp.int32),
            pltpu.SMEM((NREGION,), f32),
            pltpu.SMEM((2, HISTORY), jnp.int32),
            pltpu.VMEM((rows, 128), f32),
            pltpu.VMEM((rows, 128), jnp.int32),
            pltpu.VMEM((total + 2 * pad, 128), f32),
            pltpu.VMEM((total, 128), f32),
            pltpu.VMEM((HISTORY, 2, total, 128), jnp.bfloat16),
            pltpu.VMEM((HISTORY, 2, total, 128), jnp.bfloat16),
            pltpu.VMEM((2, total, 128), f32),
            pltpu.VMEM((HISTORY, 2, total, 128), f32),
            pltpu.VMEM((2, total + 16, 128), f32),
            pltpu.VMEM((2, HISTORY + 1, 2, ne, 128), f32),
            pltpu.VMEM((2, 2, ne, 128), f32),
            pltpu.VMEM((2, ne, 128), f32),
            pltpu.VMEM((2, ne, 128), f32),
            pltpu.VMEM((2, HISTORY + 1, 2, len(EARLY) * (ne // PIECES), 128), f32),
            pltpu.VMEM((total // (8 * TABLE), 3, 8, 128), f32),
            pltpu.VMEM((8, 128), jnp.int32),
            pltpu.VMEM((7, 8, 128), f32),
            pltpu.VMEM((2, 1, 128), f32),
            pltpu.VMEM((1, 128), f32),
            pltpu.VMEM((1, 128), f32),
            pltpu.VMEM((32, 128), f32),
            pltpu.VMEM((1, 128), f32),
            pltpu.VMEM((count, 1, 128), f32),
            pltpu.VMEM((2, HALO_PIECES, pad // HALO_PIECES, 128), f32),
            pltpu.SemaphoreType.DMA((8,)),
            pltpu.SemaphoreType.DMA((5,)),
            pltpu.SemaphoreType.DMA((2, HALO_PIECES)),
            pltpu.SemaphoreType.DMA((2, HALO_PIECES)),
            pltpu.SemaphoreType.DMA((2,)),
            pltpu.SemaphoreType.DMA((2,)),
            pltpu.SemaphoreType.DMA,
            pltpu.SemaphoreType.DMA,
            pltpu.SemaphoreType.DMA((2, PIECES)),
            pltpu.SemaphoreType.DMA((2, PIECES)),
            pltpu.SemaphoreType.DMA((2, 2, len(EARLY))),
            pltpu.SemaphoreType.DMA((2, 2, len(EARLY))),
        ],
        compiler_params=pltpu.CompilerParams(
            collective_id=0, has_side_effects=True, vmem_limit_bytes=40 << 20
        ),
    )(
        *[pltpu.with_memory_space_constraint(x, pltpu.HBM) for x in (phonon_bins, coupling, hist_used, mobility, region,
        dist.reshape(2, total, 128),
        hist_x.reshape(HISTORY, 2, total, 128),
        hist_g.reshape(HISTORY, 2, total, 128))],
    )
    return result.reshape(dist.shape)


def solution(mesh):
    in_specs = (
        P(None, "egrp", "space", None),
        P(None, None, "egrp", "space", None),
        P(None, None, "egrp", "space", None),
        P("space", None),
        P("space", None),
        P(),
        P(),
        P(),
    )
    out_specs = P(None, "egrp", "space", None)
    body = functools.partial(local, mesh.shape["egrp"], mesh.shape["space"])
    return jax.shard_map(body, mesh=mesh, in_specs=in_specs, out_specs=out_specs, check_vma=False)
```

```python
import functools
import jax
import jax.numpy as jnp
from jax import lax
from jax.experimental import pallas as pl
from jax.experimental.pallas import tpu as pltpu
from jax.sharding import PartitionSpec as P

NE = 1024
HISTORY = 4
NREGION = 4
KMAX = 64
COLS = 64
PIECES = 16
EARLY = (4, 6)
LATE = ((0, 2), (2, 4), (6, 8), (8, 10), (10, 12), (12, 14), (14, 15), (15, 16))
HALO_PIECES = 4
STEP = 32
WIDE = 128
PAIRS = [(i, j) for i in range(HISTORY + 1) for j in range(i, HISTORY + 1)]
MESH = pl.DeviceIdType.MESH


def dos_of(energy):
    value = (energy.astype(jnp.float32) + 0.5) * (1.0 / NE)
    return value * lax.rsqrt(value)


def solve(total, field, used_ref):
    def entry(i, j):
        lane = field * len(PAIRS) + PAIRS.index((min(i, j), max(i, j)))
        return jnp.broadcast_to(total[:, lane : lane + 1], (8, 128))

    size = HISTORY + 1
    valid = [jnp.ones((8, 128), jnp.float32)]
    for index in range(HISTORY):
        valid.append(jnp.full((8, 128), used_ref[field, index].astype(jnp.float32)))
    first = entry(0, 0)
    low = [[None] * size for _ in range(size)]
    scaled = [[None] * size for _ in range(size)]
    inverse = [None] * size
    for j in range(size):
        for i in range(j, size):
            value = valid[i] * valid[j] * entry(i, j)
            if i == j:
                value = value + (1.0 - valid[i]) * first
            for k in range(j):
                value = value - scaled[i][k] * low[j][k]
            scaled[i][j] = value
        inverse[j] = 1.0 / scaled[j][j]
        for i in range(j + 1, size):
            low[i][j] = scaled[i][j] * inverse[j]
    forward = []
    for i in range(size):
        value = valid[i]
        for k in range(i):
            value = value - low[i][k] * forward[k]
        forward.append(value)
    weights = [None] * size
    for i in reversed(range(size)):
        value = forward[i] * inverse[i]
        for k in range(i + 1, size):
            value = value - low[k][i] * weights[k]
        weights[i] = value
    inv_sum = 1.0 / functools.reduce(lambda a, b: a + b, weights)
    return [w * inv_sum for w in weights]


def kernel(
    n_egrp, n_space, ne, rows,
    bins_hbm, coup_hbm, used_hbm, mob_hbm, region_hbm, dist_hbm, hx_hbm, hg_hbm,
    out,
    bins_ref, coup_ref, used_ref, mob_ref, region_ref,
    even, odd, hg, hx, base, hist, mixed, edges, lo, hi, ahead, cell, tile, across, weight,
    mob_send, mob_lo, mob_hi, sums, part, gathered, halo,
    in_sem, small_sem, halo_send, halo_recv, mob_ssem, mob_rsem, sum_send, sum_recv,
    edge_send, edge_recv, ahead_send, ahead_recv,
):
    my_e = lax.axis_index("egrp")
    my_s = lax.axis_index("space")
    count = n_egrp * n_space
    me = my_e * n_space + my_s
    total_rows = ne * rows
    pad = KMAX * rows
    group = 8 // rows
    piece = ne // PIECES
    first_early, last_early = EARLY[0] * piece, EARLY[1] * piece
    early = pl.ds(first_early, last_early - first_early)

    def device(index):
        return (index // n_space, lax.rem(index, n_space))

    small = [
        pltpu.make_async_copy(source, target, small_sem.at[index])
        for index, (source, target) in enumerate((
            (region_hbm, region_ref), (bins_hbm, bins_ref), (coup_hbm, coup_ref),
            (mob_hbm, mob_ref), (used_hbm, used_ref),
        ))
    ]
    cuts = [0, first_early * rows, last_early * rows, total_rows]
    parts = [pl.ds(cuts[index], cuts[index + 1] - cuts[index]) for index in range(3)]

    def history_load(source, target, index, sem):
        return pltpu.make_async_copy(
            source.at[:, :, parts[index]], target.at[:, :, parts[index]], in_sem.at[sem]
        )

    first = [history_load(hx_hbm, hx, 1, 2), history_load(hg_hbm, hg, 1, 3)]
    older = [history_load(hg_hbm, hg, 2, 4), history_load(hg_hbm, hg, 0, 5)]
    loads = [
        pltpu.make_async_copy(dist_hbm.at[0], even.at[pl.ds(pad, total_rows)], in_sem.at[0]),
        pltpu.make_async_copy(dist_hbm.at[1], odd, in_sem.at[1]),
    ]
    late = [history_load(hx_hbm, hx, 0, 6), history_load(hx_hbm, hx, 2, 7)]
    for copy in small + first + older + loads + late:
        copy.start()

    barrier = pltpu.get_barrier_semaphore()

    def greet(step, carry):
        pl.semaphore_signal(
            barrier, inc=1, device_id=device(lax.rem(me + step, count)), device_id_type=MESH
        )
        return carry

    lax.fori_loop(n_space, count, greet, 0)
    lax.fori_loop(1, n_space, greet, 0)

    has_below_e = my_e > 0
    has_above_e = my_e < n_egrp - 1
    has_below = my_s > 0
    has_above = my_s < n_space - 1

    for copy in small:
        copy.wait()
    for copy_of in range(group):
        tile[pl.ds(copy_of * rows, rows), :] = region_ref[...]
    mob_send[0] = mob_ref[0:1, :]
    mob_send[1] = mob_ref[rows - 1 : rows, :]

    even[pl.ds(0, pad), :] = jnp.zeros((pad, 128), jnp.float32)
    even[pl.ds(pad + total_rows, pad), :] = jnp.zeros((pad, 128), jnp.float32)

    @pl.when(my_s == 0)
    def _():
        lo[...] = jnp.zeros(lo.shape, jnp.float32)
        ahead[0] = jnp.zeros(ahead.shape[1:], jnp.float32)
        mob_lo[...] = jnp.zeros(mob_lo.shape, jnp.float32)

    @pl.when(my_s == n_space - 1)
    def _():
        hi[...] = jnp.zeros(hi.shape, jnp.float32)
        ahead[1] = jnp.zeros(ahead.shape[1:], jnp.float32)
        mob_hi[...] = jnp.zeros(mob_hi.shape, jnp.float32)

    sums[...] = jnp.zeros(sums.shape, jnp.float32)
    pl.semaphore_wait(barrier, count - 1)

    chunk = pad // HALO_PIECES
    halos = []
    for index in range(HALO_PIECES):
        up_e = pltpu.make_async_remote_copy(
            dist_hbm.at[0, pl.ds(total_rows - pad + index * chunk, chunk)],
            halo.at[0, index],
            halo_send.at[0, index], halo_recv.at[0, index],
            device_id=(lax.rem(my_e + 1, n_egrp), my_s), device_id_type=MESH,
        )
        down_e = pltpu.make_async_remote_copy(
            dist_hbm.at[0, pl.ds(index * chunk, chunk)],
            halo.at[1, index],
            halo_send.at[1, index], halo_recv.at[1, index],
            device_id=(lax.rem(my_e + n_egrp - 1, n_egrp), my_s), device_id_type=MESH,
        )
        halos.append((up_e, down_e))
    next_s = lax.rem(my_s + 1, n_space)
    prev_s = lax.rem(my_s + n_space - 1, n_space)

    def pair(up_source, up_target, down_source, down_target, send, recv):
        return (
            pltpu.make_async_remote_copy(
                up_source, up_target, send[0], recv[0],
                device_id=(my_e, next_s), device_id_type=MESH,
            ),
            pltpu.make_async_remote_copy(
                down_source, down_target, send[1], recv[1],
                device_id=(my_e, prev_s), device_id_type=MESH,
            ),
        )

    def start(copies):
        @pl.when(has_above)
        def _():
            copies[0].start()

        @pl.when(has_below)
        def _():
            copies[1].start()

    def arrive(copies):
        @pl.when(has_below)
        def _():
            copies[0].wait_recv()

        @pl.when(has_above)
        def _():
            copies[1].wait_recv()

    mobs = pair(
        mob_send.at[1], mob_lo, mob_send.at[0], mob_hi,
        [mob_ssem.at[0], mob_ssem.at[1]], [mob_rsem.at[0], mob_rsem.at[1]],
    )

    @pl.when(has_above_e)
    def _():
        for up_e, _ in halos:
            up_e.start()

    @pl.when(has_below_e)
    def _():
        for _, down_e in halos:
            down_e.start()

    start(mobs)

    def join_history(step, carry):
        row = pl.multiple_of(step * STEP, STEP)
        for index in range(HISTORY):
            for field in range(2):
                hist[index, field, pl.ds(row, STEP), :] = hx[
                    index, field, pl.ds(row, STEP), :
                ].astype(jnp.float32) + 0.5 * hg[index, field, pl.ds(row, STEP), :].astype(
                    jnp.float32
                )
        return carry

    def pack(terms, step, carry):
        at = pl.multiple_of(step * 8, 8)
        for field in range(2):
            for side, row in ((0, 0), (1, rows - 1)):
                for term in terms:
                    source = pl.ds((first_early + at) * rows + row, 8, stride=rows)
                    value = (
                        base[field, source, :] if term == 0 else hist[term - 1, field, source, :]
                    )
                    edges[side, term, field, pl.ds(at, 8), :] = value
        return carry

    def send_ahead(terms, kind):
        lax.fori_loop(0, (last_early - first_early) // 8, functools.partial(pack, terms), 0)
        at = pl.ds(terms[0], len(terms))
        copies = pair(
            edges.at[1, at], ahead.at[0, at], edges.at[0, at], ahead.at[1, at],
            [ahead_send.at[side, kind] for side in range(2)],
            [ahead_recv.at[side, kind] for side in range(2)],
        )
        start(copies)
        return copies

    for copy in first:
        copy.wait()
    lax.fori_loop(cuts[1] // STEP, cuts[2] // STEP, join_history, 0)
    early_sends = [send_ahead(tuple(range(1, HISTORY + 1)), 0)]

    def older_pairs(step, accs):
        row = pl.multiple_of(step * STEP, STEP)
        new = []
        for field in range(2):
            vectors = [
                hg[index, field, pl.ds(row, STEP), :].astype(jnp.float32)
                for index in range(HISTORY)
            ]
            for i, j in PAIRS:
                if i > 0:
                    value = accs[len(new)]
                    for sub in range(STEP // 8):
                        at = slice(sub * 8, sub * 8 + 8)
                        value = value + vectors[i - 1][at] * vectors[j - 1][at]
                    new.append(value)
        return tuple(new)

    for copy in older:
        copy.wait()
    zero = jnp.zeros((8, 128), jnp.float32)
    n_older = len(PAIRS) - HISTORY - 1
    older_accs = lax.fori_loop(0, total_rows // STEP, older_pairs, (zero,) * (2 * n_older))
    for position, acc in enumerate(older_accs):
        at = (position // n_older) * len(PAIRS) + HISTORY + 1 + position % n_older
        sums[at : at + 1, :] = jnp.sum(acc, axis=0, keepdims=True)

    region = tile[...]
    bins = jnp.zeros((8, 128), jnp.int32)
    lam = jnp.zeros((8, 128), jnp.float32)
    for index in range(NREGION):
        bins = jnp.where(region == index, bins_ref[index], bins)
        lam = jnp.where(region == index, coup_ref[index], lam)
    inner = (lax.broadcasted_iota(jnp.int32, (8, 128), 0) // rows).astype(jnp.float32) + 0.5
    reach = bins.astype(jnp.float32)
    for place, value in enumerate((
        inner, inner - reach, inner + reach, lam,
        lam * (1.5 * NE**-0.5), lam * (0.5 * NE**-0.5),
    )):
        cell[place] = value

    for copy in loads:
        copy.wait()

    subs = STEP // 8

    def residuals(step, accs):
        row = pl.multiple_of(step * STEP, STEP)
        region = tile[...]
        chosen = [region == index for index in range(1, NREGION)]
        inner, low, high, lam, most, least = [cell[place] for place in range(6)]
        above, below = [], []
        for index in range(NREGION):
            shift = bins_ref[index] * rows
            up = even[pl.ds(pad + row + shift, STEP), :]
            down = even[pl.ds(pad + row - shift, STEP), :]
            for sub in range(subs):
                at = slice(sub * 8, sub * 8 + 8)
                if index == 0:
                    above.append(up[at])
                    below.append(down[at])
                else:
                    above[sub] = jnp.where(chosen[index - 1], up[at], above[sub])
                    below[sub] = jnp.where(chosen[index - 1], down[at], below[sub])
        own_even = even[pl.ds(pad + row, STEP), :]
        own_odd = odd[pl.ds(row, STEP), :]
        res = [[], []]
        for sub in range(subs):
            at = slice(sub * 8, sub * 8 + 8)
            level = (my_e * ne + step * (STEP // rows) + sub * group).astype(jnp.float32)
            lower = level + low
            upper = level + high
            middle = level + inner
            root_low = jnp.maximum(lower, 0.0) * lax.rsqrt(jnp.maximum(lower, 0.25))
            root_high = jnp.where(upper < NE, upper * lax.rsqrt(upper), 0.0)
            loss = 1.0 + (most * root_low + least * root_high)
            more = loss + lam
            both = 1.0 / (loss * more)
            gain = (least * (middle * lax.rsqrt(middle))) * (3.0 * above[sub] + below[sub])
            res[0].append((own_even[at] + gain) * (both * more) - own_even[at])
            res[1].append(own_odd[at] * (both * loss) - own_odd[at])
            base[0, pl.ds(row + sub * 8, 8), :] = own_even[at] + 0.5 * res[0][sub]
            base[1, pl.ds(row + sub * 8, 8), :] = own_odd[at] + 0.5 * res[1][sub]
        new = []
        for field in range(2):
            for index in range(HISTORY + 1):
                value = accs[len(new)]
                if index > 0:
                    other = hg[index - 1, field, pl.ds(row, STEP), :].astype(jnp.float32)
                for sub in range(subs):
                    at = slice(sub * 8, sub * 8 + 8)
                    value = value + res[field][sub] * (other[at] if index > 0 else res[field][sub])
                new.append(value)
        return tuple(new)

    accs = (zero,) * (2 * (HISTORY + 1))
    edge = pad // STEP
    steps = total_rows // STEP
    first_free = jnp.where(has_below_e, edge, 0)
    last_free = jnp.where(has_above_e, steps - edge, steps)
    accs = lax.fori_loop(first_free, last_free, residuals, accs)

    stride = edge // HALO_PIECES
    for index in range(HALO_PIECES):
        @pl.when(has_below_e)
        def _():
            halos[index][0].wait_recv()
            even[pl.ds(index * chunk, chunk), :] = halo[0, index]

        if index == 0:
            continue
        stop = edge if index == HALO_PIECES - 1 else index * stride
        accs = lax.fori_loop(
            jnp.where(has_below_e, (index - 1) * stride, 0),
            jnp.where(has_below_e, stop, 0), residuals, accs,
        )
    for index in range(HALO_PIECES):
        @pl.when(has_above_e)
        def _():
            halos[index][1].wait_recv()
            even[pl.ds(pad + total_rows + index * chunk, chunk), :] = halo[1, index]

        accs = lax.fori_loop(
            jnp.where(has_above_e, steps - edge + index * stride, steps),
            jnp.where(has_above_e, steps - edge + (index + 1) * stride, steps), residuals, accs,
        )

    for position, acc in enumerate(accs):
        at = (position // (HISTORY + 1)) * len(PAIRS) + position % (HISTORY + 1)
        sums[at : at + 1, :] = jnp.sum(acc, axis=0, keepdims=True)
    lane_sum = jnp.sum(sums[...], axis=1, keepdims=True)
    place = lax.broadcasted_iota(jnp.int32, sums.shape, 0) == lax.broadcasted_iota(
        jnp.int32, sums.shape, 1
    )
    row_sum = jnp.sum(jnp.where(place, lane_sum, 0.0), axis=0, keepdims=True)
    part[...] = row_sum
    gathered[me] = row_sum

    def send_sums(step, carry):
        pltpu.make_async_remote_copy(
            part, gathered.at[me], sum_send, sum_recv,
            device_id=device(lax.rem(me + step, count)), device_id_type=MESH,
        ).start()
        return carry

    lax.fori_loop(1, count, send_sums, 0)

    early_sends.append(send_ahead((0,), 1))

    for copy in late:
        copy.wait()
    lax.fori_loop(0, cuts[1] // STEP, join_history, 0)
    lax.fori_loop(cuts[2] // STEP, steps, join_history, 0)

    arrive(mobs)

    lanes = lax.broadcasted_iota(jnp.int32, (1, 128), 1)
    column = lanes % COLS
    for row in range(rows):
        mob = mob_ref[row : row + 1, :]
        under = mob_lo[...] if row == 0 else mob_ref[row - 1 : row, :]
        over = mob_hi[...] if row == rows - 1 else mob_ref[row + 1 : row + 2, :]
        w_under = 0.04 * (mob + under)
        w_over = 0.04 * (mob + over)
        if row == 0:
            w_under = jnp.where(has_below, w_under, 0.0)
        if row == rows - 1:
            w_over = jnp.where(has_above, w_over, 0.0)
        w_left = jnp.where(column > 0, 0.04 * (mob + pltpu.roll(mob, 1, 1)), 0.0)
        w_right = jnp.where(column < COLS - 1, 0.04 * (mob + pltpu.roll(mob, 127, 1)), 0.0)
        w_plane = 0.04 * (mob + pltpu.roll(mob, COLS, 1))
        own = 1.0 - (w_under + w_over + w_left + w_right + w_plane)
        weight[0, row] = jnp.broadcast_to(w_under, (8, 128))
        weight[1, row] = jnp.broadcast_to(w_over, (8, 128))
        to = lax.broadcasted_iota(jnp.int32, (128, 128), 1)
        gap = to - lax.broadcasted_iota(jnp.int32, (128, 128), 0)
        matrix = jnp.where(gap == 0, own, 0.0)
        matrix = jnp.where(gap == 1, w_left, matrix)
        matrix = jnp.where(gap == -1, w_right, matrix)
        matrix = jnp.where((gap == COLS) | (gap == -COLS), w_plane, matrix)
        main = matrix.astype(jnp.bfloat16)
        rest = (matrix - main.astype(jnp.float32)).astype(jnp.bfloat16)
        across[row, pl.ds(0, 128), pl.ds(0, 128)] = main
        across[row, pl.ds(128, 128), pl.ds(0, 128)] = main
        across[row, pl.ds(0, 128), pl.ds(128, 128)] = rest
        across[row, pl.ds(128, 128), pl.ds(128, 128)] = jnp.zeros((128, 128), jnp.bfloat16)

    sums_in = gathered.at[pl.ds(0, count - 1)]
    pltpu.make_async_copy(sums_in, sums_in, sum_recv).wait()
    total = jnp.sum(gathered[...], axis=0)
    narrow = [solve(total, field, used_ref) for field in range(2)]

    def mix(which, step, carry):
        at = pl.multiple_of(step * 8, 8)
        for field in range(2):
            for row in which:
                source = pl.ds(at * rows + row, 8, stride=rows)
                value = narrow[field][0] * base[field, source, :]
                for index in range(HISTORY):
                    value = value + narrow[field][index + 1] * hist[index, field, source, :]
                mixed[field, row, pl.ds(at, 8), :] = value
        return carry

    outer = functools.partial(mix, (0, rows - 1))
    sends = []
    for index, (begin, end) in enumerate(LATE):
        lax.fori_loop(begin * (piece // 8), end * (piece // 8), outer, 0)
        span = pl.ds(begin * piece, (end - begin) * piece)
        copies = pair(
            mixed.at[:, rows - 1, span], lo.at[:, span], mixed.at[:, 0, span], hi.at[:, span],
            [edge_send.at[side, index] for side in range(2)],
            [edge_recv.at[side, index] for side in range(2)],
        )
        start(copies)
        sends.append(copies)

    lax.fori_loop(first_early // 8, last_early // 8, outer, 0)
    lax.fori_loop(0, ne // 8, functools.partial(mix, tuple(range(1, rows - 1))), 0)

    wide = min(WIDE, ne)

    def drift(block, carry):
        first = pl.multiple_of(block * wide, wide)
        at = pl.ds(first, wide)
        level = (
            (my_e * ne + first).astype(jnp.float32) + 0.5
            + lax.broadcasted_iota(jnp.int32, (wide, 128), 0).astype(jnp.float32)
        ) * (1.0 / NE)
        drive = 0.25 * (level * lax.rsqrt(level))
        for row in range(rows):
            for field in range(2):
                value = mixed[field, row, at, :]
                main = value.astype(jnp.bfloat16)
                rest = (value - main.astype(jnp.float32)).astype(jnp.bfloat16)
                both = jnp.dot(
                    jnp.concatenate([main, rest], axis=1), across[row],
                    preferred_element_type=jnp.float32,
                )
                result = both[:, :128] + both[:, 128:]
                if row > 0:
                    result = result + weight[0, row, 0:1, :] * mixed[field, row - 1, at, :]
                if row < rows - 1:
                    result = result + weight[1, row, 0:1, :] * mixed[field, row + 1, at, :]
                coupled = drive * mixed[1 - field, row, at, :]
                result = result + coupled if field == 0 else result - coupled
                out[field, pl.ds(first * rows + row, wide, stride=rows), :] = result
        return carry

    lax.fori_loop(0, ne // wide, drift, 0)

    def add_edges(step, carry):
        at = pl.multiple_of(step * 8, 8)
        for field in range(2):
            for row, edge_of, kind in ((0, lo, 0), (rows - 1, hi, 1)):
                to = pl.ds(at * rows + row, 8, stride=rows)
                out[field, to, :] = (
                    out[field, to, :] + weight[kind, row] * edge_of[field, pl.ds(at, 8), :]
                )
        return carry

    for copies in early_sends:
        arrive(copies)

    def mix_early(step, carry):
        at = pl.multiple_of(step * 8, 8)
        for side, target in ((0, lo), (1, hi)):
            for field in range(2):
                value = narrow[field][0] * ahead[side, 0, field, pl.ds(at, 8), :]
                for term in range(1, HISTORY + 1):
                    value = value + narrow[field][term] * ahead[side, term, field, pl.ds(at, 8), :]
                target[field, pl.ds(first_early + at, 8), :] = value
        return carry

    lax.fori_loop(0, (last_early - first_early) // 8, mix_early, 0)
    lax.fori_loop(first_early // 8, last_early // 8, add_edges, 0)

    for (begin, end), copies in zip(LATE, sends):
        arrive(copies)
        lax.fori_loop(begin * (piece // 8), end * (piece // 8), add_edges, 0)

    sums_out = gathered.at[pl.ds(0, count - 1)]
    pltpu.make_async_copy(sums_out, sums_out, sum_send).wait()

    @pl.when(has_above_e)
    def _():
        for up_e, _ in halos:
            up_e.wait_send()

    @pl.when(has_below_e)
    def _():
        for _, down_e in halos:
            down_e.wait_send()

    sent = [mobs] + early_sends + sends

    @pl.when(has_above)
    def _():
        for up, _ in sent:
            up.wait_send()

    @pl.when(has_below)
    def _():
        for _, down in sent:
            down.wait_send()


def local(n_egrp, n_space, dist, hist_x, hist_g, mobility, region, phonon_bins, coupling, hist_used):
    ne, rows = dist.shape[1], dist.shape[2]
    total = ne * rows
    pad = KMAX * rows
    count = n_egrp * n_space
    early = (EARLY[1] - EARLY[0]) * (ne // PIECES)
    f32 = jnp.float32
    vmem = pl.BlockSpec(memory_space=pltpu.VMEM)
    hbm = pl.BlockSpec(memory_space=pltpu.HBM)
    result = pl.pallas_call(
        functools.partial(kernel, n_egrp, n_space, ne, rows),
        out_shape=jax.ShapeDtypeStruct((2, total, 128), f32),
        in_specs=[hbm] * 8,
        out_specs=vmem,
        scratch_shapes=[
            pltpu.SMEM((NREGION,), jnp.int32),
            pltpu.SMEM((NREGION,), f32),
            pltpu.SMEM((2, HISTORY), jnp.int32),
            pltpu.VMEM((rows, 128), f32),
            pltpu.VMEM((rows, 128), jnp.int32),
            pltpu.VMEM((total + 2 * pad, 128), f32),
            pltpu.VMEM((total, 128), f32),
            pltpu.VMEM((HISTORY, 2, total, 128), jnp.bfloat16),
            pltpu.VMEM((HISTORY, 2, total, 128), jnp.bfloat16),
            pltpu.VMEM((2, total, 128), f32),
            pltpu.VMEM((HISTORY, 2, total, 128), f32),
            pltpu.VMEM((2, rows, ne, 128), f32),
            pltpu.VMEM((2, HISTORY + 1, 2, early, 128), f32),
            pltpu.VMEM((2, ne, 128), f32),
            pltpu.VMEM((2, ne, 128), f32),
            pltpu.VMEM((2, HISTORY + 1, 2, early, 128), f32),
            pltpu.VMEM((6, 8, 128), f32),
            pltpu.VMEM((8, 128), jnp.int32),
            pltpu.VMEM((rows, 256, 256), jnp.bfloat16),
            pltpu.VMEM((2, rows, 8, 128), f32),
            pltpu.VMEM((2, 1, 128), f32),
            pltpu.VMEM((1, 128), f32),
            pltpu.VMEM((1, 128), f32),
            pltpu.VMEM((32, 128), f32),
            pltpu.VMEM((1, 128), f32),
            pltpu.VMEM((count, 1, 128), f32),
            pltpu.VMEM((2, HALO_PIECES, pad // HALO_PIECES, 128), f32),
            pltpu.SemaphoreType.DMA((8,)),
            pltpu.SemaphoreType.DMA((5,)),
            pltpu.SemaphoreType.DMA((2, HALO_PIECES)),
            pltpu.SemaphoreType.DMA((2, HALO_PIECES)),
            pltpu.SemaphoreType.DMA((2,)),
            pltpu.SemaphoreType.DMA((2,)),
            pltpu.SemaphoreType.DMA,
            pltpu.SemaphoreType.DMA,
            pltpu.SemaphoreType.DMA((2, len(LATE))),
            pltpu.SemaphoreType.DMA((2, len(LATE))),
            pltpu.SemaphoreType.DMA((2, 2)),
            pltpu.SemaphoreType.DMA((2, 2)),
        ],
        compiler_params=pltpu.CompilerParams(
            collective_id=0, has_side_effects=True, vmem_limit_bytes=40 << 20
        ),
    )(
        *[pltpu.with_memory_space_constraint(x, pltpu.HBM) for x in (phonon_bins, coupling, hist_used, mobility, region,
        dist.reshape(2, total, 128),
        hist_x.reshape(HISTORY, 2, total, 128),
        hist_g.reshape(HISTORY, 2, total, 128))],
    )
    return result.reshape(dist.shape)


def solution(mesh):
    in_specs = (
        P(None, "egrp", "space", None),
        P(None, None, "egrp", "space", None),
        P(None, None, "egrp", "space", None),
        P("space", None),
        P("space", None),
        P(),
        P(),
        P(),
    )
    out_specs = P(None, "egrp", "space", None)
    body = functools.partial(local, mesh.shape["egrp"], mesh.shape["space"])
    return jax.shard_map(body, mesh=mesh, in_specs=in_specs, out_specs=out_specs, check_vma=False)
```

```python
import functools
import jax
import jax.numpy as jnp
from jax import lax
from jax.experimental import pallas as pl
from jax.experimental.pallas import tpu as pltpu
from jax.sharding import PartitionSpec as P

NE = 1024
HISTORY = 4
NREGION = 4
KMAX = 64
COLS = 64
PIECES = 16
RELAYS = (0, 1, 3, 4)
HALO_PIECES = 4
JOIN = 32
STEP = 64
WIDE = 128
PAIRS = [(i, j) for i in range(HISTORY + 1) for j in range(i, HISTORY + 1)]
MESH = pl.DeviceIdType.MESH


def dos_of(energy):
    value = (energy.astype(jnp.float32) + 0.5) * (1.0 / NE)
    return value * lax.rsqrt(value)


def plan(ne):
    piece = ne // PIECES
    ahead = (4 * piece, 6 * piece, 6 * piece + max(8, 3 * piece // 4))
    cuts = [ahead[2]] + [index * piece for index in (8, 9, 11, 13, 15, 16)]
    late = [(0, 3 * piece), (3 * piece, 4 * piece)] + list(zip(cuts[:-1], cuts[1:]))
    return ahead, late


def solve(total, field, used_ref):
    def entry(i, j):
        lane = field * len(PAIRS) + PAIRS.index((min(i, j), max(i, j)))
        return jnp.broadcast_to(total[:, lane : lane + 1], (8, 128))

    size = HISTORY + 1
    valid = [jnp.ones((8, 128), jnp.float32)]
    for index in range(HISTORY):
        valid.append(jnp.full((8, 128), used_ref[field, index].astype(jnp.float32)))
    first = entry(0, 0)
    low = [[None] * size for _ in range(size)]
    scaled = [[None] * size for _ in range(size)]
    inverse = [None] * size
    for j in range(size):
        for i in range(j, size):
            value = valid[i] * valid[j] * entry(i, j)
            if i == j:
                value = value + (1.0 - valid[i]) * first
            for k in range(j):
                value = value - scaled[i][k] * low[j][k]
            scaled[i][j] = value
        inverse[j] = 1.0 / scaled[j][j]
        for i in range(j + 1, size):
            low[i][j] = scaled[i][j] * inverse[j]
    forward = []
    for i in range(size):
        value = valid[i]
        for k in range(i):
            value = value - low[i][k] * forward[k]
        forward.append(value)
    weights = [None] * size
    for i in reversed(range(size)):
        value = forward[i] * inverse[i]
        for k in range(i + 1, size):
            value = value - low[k][i] * weights[k]
        weights[i] = value
    inv_sum = 1.0 / functools.reduce(lambda a, b: a + b, weights)
    return [w * inv_sum for w in weights]


def kernel(
    n_egrp, n_space, ne, rows,
    bins_hbm, coup_hbm, used_hbm, mob_hbm, region_hbm, dist_hbm, hx_hbm, hg_hbm,
    out,
    bins_ref, coup_ref, used_ref, mob_ref, region_ref,
    even, odd, hg, hx, base, hist, mixed, edges, lo, hi, ahead, cell, tile, across, weight, passed,
    mob_send, mob_lo, mob_hi, sums, part, gathered, halo,
    in_sem, small_sem, halo_send, halo_recv, mob_ssem, mob_rsem, sum_send, sum_recv,
    edge_send, edge_recv, ahead_send, ahead_recv, relay_send, relay_recv, pass_send,
):
    my_e = lax.axis_index("egrp")
    my_s = lax.axis_index("space")
    count = n_egrp * n_space
    me = my_e * n_space + my_s
    total_rows = ne * rows
    pad = KMAX * rows
    group = 8 // rows
    (first_early, last_early, end_early), late_spans = plan(ne)

    def device(index):
        return (index // n_space, lax.rem(index, n_space))

    paired = count <= 64 and n_egrp & (n_egrp - 1) == 0 and n_space & (n_space - 1) == 0
    order = sorted(range(1, count), key=lambda index: -bin(index).count("1")) if paired else []

    def partner(index):
        return (my_e ^ (index // n_space), my_s ^ (index % n_space))

    small = [
        pltpu.make_async_copy(source, target, small_sem.at[index])
        for index, (source, target) in enumerate((
            (region_hbm, region_ref), (bins_hbm, bins_ref), (coup_hbm, coup_ref),
            (mob_hbm, mob_ref), (used_hbm, used_ref),
        ))
    ]
    cuts = [0, first_early * rows, last_early * rows, total_rows]
    parts = [pl.ds(cuts[index], cuts[index + 1] - cuts[index]) for index in range(3)]

    def history_load(source, target, index, sem):
        return pltpu.make_async_copy(
            source.at[:, :, parts[index]], target.at[:, :, parts[index]], in_sem.at[sem]
        )

    first = [history_load(hx_hbm, hx, 1, 2), history_load(hg_hbm, hg, 1, 3)]
    older = [history_load(hg_hbm, hg, 2, 4), history_load(hg_hbm, hg, 0, 5)]
    loads = [
        pltpu.make_async_copy(dist_hbm.at[0], even.at[pl.ds(pad, total_rows)], in_sem.at[0]),
        pltpu.make_async_copy(dist_hbm.at[1], odd, in_sem.at[1]),
    ]
    late = [history_load(hx_hbm, hx, 0, 6), history_load(hx_hbm, hx, 2, 7)]
    barrier = pltpu.get_barrier_semaphore()

    def greet(step, carry):
        pl.semaphore_signal(
            barrier, inc=1, device_id=device(lax.rem(me + step, count)), device_id_type=MESH
        )
        return carry

    if paired:
        for index in [n_space] + [index for index in order if index != n_space]:
            pl.semaphore_signal(barrier, inc=1, device_id=partner(index), device_id_type=MESH)
    else:
        lax.fori_loop(n_space, count, greet, 0)
        lax.fori_loop(1, n_space, greet, 0)
    for copy in small + first + older + loads + late:
        copy.start()

    has_below_e = my_e > 0
    has_above_e = my_e < n_egrp - 1
    has_below = my_s > 0
    has_above = my_s < n_space - 1

    for copy in small:
        copy.wait()
    for copy_of in range(group):
        tile[pl.ds(copy_of * rows, rows), :] = region_ref[...]
    mob_send[0] = mob_ref[0:1, :]
    mob_send[1] = mob_ref[rows - 1 : rows, :]

    sums[...] = jnp.zeros(sums.shape, jnp.float32)
    pl.semaphore_wait(barrier, count - 1)

    chunk = pad // HALO_PIECES
    halos = []
    for index in range(HALO_PIECES):
        up_e = pltpu.make_async_remote_copy(
            dist_hbm.at[0, pl.ds(total_rows - pad + index * chunk, chunk)],
            halo.at[0, index],
            halo_send.at[0, index], halo_recv.at[0, index],
            device_id=(lax.rem(my_e + 1, n_egrp), my_s), device_id_type=MESH,
        )
        down_e = pltpu.make_async_remote_copy(
            dist_hbm.at[0, pl.ds(index * chunk, chunk)],
            halo.at[1, index],
            halo_send.at[1, index], halo_recv.at[1, index],
            device_id=(lax.rem(my_e + n_egrp - 1, n_egrp), my_s), device_id_type=MESH,
        )
        halos.append((up_e, down_e))
    next_s = lax.rem(my_s + 1, n_space)
    prev_s = lax.rem(my_s + n_space - 1, n_space)

    def pair(up_source, up_target, down_source, down_target, send, recv):
        return (
            pltpu.make_async_remote_copy(
                up_source, up_target, send[0], recv[0],
                device_id=(my_e, next_s), device_id_type=MESH,
            ),
            pltpu.make_async_remote_copy(
                down_source, down_target, send[1], recv[1],
                device_id=(my_e, prev_s), device_id_type=MESH,
            ),
        )

    def start(copies):
        @pl.when(has_above)
        def _():
            copies[0].start()

        @pl.when(has_below)
        def _():
            copies[1].start()

    def arrive(copies):
        @pl.when(has_below)
        def _():
            copies[0].wait_recv()

        @pl.when(has_above)
        def _():
            copies[1].wait_recv()

    mobs = pair(
        mob_send.at[1], mob_lo, mob_send.at[0], mob_hi,
        [mob_ssem.at[0], mob_ssem.at[1]], [mob_rsem.at[0], mob_rsem.at[1]],
    )

    @pl.when(has_above_e)
    def _():
        for up_e, _ in halos:
            up_e.start()

    @pl.when(has_below_e)
    def _():
        for _, down_e in halos:
            down_e.start()

    start(mobs)

    even[pl.ds(0, pad), :] = jnp.zeros((pad, 128), jnp.float32)
    even[pl.ds(pad + total_rows, pad), :] = jnp.zeros((pad, 128), jnp.float32)

    def join_history(step, carry):
        row = pl.multiple_of(step * JOIN, JOIN)
        for index in range(HISTORY):
            for field in range(2):
                hist[index, field, pl.ds(row, JOIN), :] = hx[
                    index, field, pl.ds(row, JOIN), :
                ].astype(jnp.float32) + 0.5 * hg[index, field, pl.ds(row, JOIN), :].astype(
                    jnp.float32
                )
        return carry

    def join_current(step, carry):
        row = pl.multiple_of(step * JOIN, JOIN)
        at = pl.ds(row, JOIN)
        base[0, at, :] = 0.5 * (even[pl.ds(pad + row, JOIN), :] + base[0, at, :])
        base[1, at, :] = 0.5 * (odd[at, :] + base[1, at, :])
        return carry

    def pack(terms, step, carry):
        at = pl.multiple_of(step * 8, 8)
        for field in range(2):
            for side, row in ((0, 0), (1, rows - 1)):
                for term in terms:
                    source = pl.ds((first_early + at) * rows + row, 8, stride=rows)
                    if term == 0:
                        shift = pad if field == 0 else 0
                        own = pl.ds(shift + (first_early + at) * rows + row, 8, stride=rows)
                        value = 0.5 * ((odd if field else even)[own, :] + base[field, source, :])
                    else:
                        value = hist[term - 1, field, source, :]
                    edges[side, term, field, pl.ds(at, 8), :] = value
        return carry

    def send_ahead(terms, begin, end, kind):
        at, to = pl.ds(begin - first_early, end - begin), pl.ds(terms[0], len(terms))
        lax.fori_loop(
            (begin - first_early) // 8, (end - first_early) // 8, functools.partial(pack, terms), 0
        )
        copies = pair(
            edges.at[1, to, :, at], ahead.at[0, to, :, at],
            edges.at[0, to, :, at], ahead.at[1, to, :, at],
            [ahead_send.at[side, kind] for side in range(2)],
            [ahead_recv.at[side, kind] for side in range(2)],
        )
        start(copies)
        return copies

    for copy in first:
        copy.wait()
    lax.fori_loop(cuts[1] // JOIN, cuts[2] // JOIN, join_history, 0)
    early_sends = [send_ahead(tuple(range(1, HISTORY + 1)), first_early, last_early, 0)]

    def older_pairs(step, accs):
        row = pl.multiple_of(step * STEP, STEP)
        new = []
        for field in range(2):
            vectors = [
                hg[index, field, pl.ds(row, STEP), :].astype(jnp.float32)
                for index in range(HISTORY)
            ]
            for i, j in PAIRS:
                if i > 0:
                    value = accs[len(new)]
                    for sub in range(STEP // 8):
                        at = slice(sub * 8, sub * 8 + 8)
                        value = value + vectors[i - 1][at] * vectors[j - 1][at]
                    new.append(value)
        return tuple(new)

    for copy in older:
        copy.wait()
    zero = jnp.zeros((8, 128), jnp.float32)
    n_older = len(PAIRS) - HISTORY - 1
    older_accs = lax.fori_loop(0, total_rows // STEP, older_pairs, (zero,) * (2 * n_older))
    for position, acc in enumerate(older_accs):
        at = (position // n_older) * len(PAIRS) + HISTORY + 1 + position % n_older
        sums[at : at + 1, :] = jnp.sum(acc, axis=0, keepdims=True)

    region = tile[...]
    bins = jnp.zeros((8, 128), jnp.int32)
    lam = jnp.zeros((8, 128), jnp.float32)
    for index in range(NREGION):
        bins = jnp.where(region == index, bins_ref[index], bins)
        lam = jnp.where(region == index, coup_ref[index], lam)
    inner = (lax.broadcasted_iota(jnp.int32, (8, 128), 0) // rows).astype(jnp.float32) + 0.5
    reach = bins.astype(jnp.float32)
    for place, value in enumerate((
        inner, inner - reach, inner + reach, lam,
        lam * (1.5 * NE**-0.5), lam * (0.5 * NE**-0.5),
    )):
        cell[place] = value

    for copy in loads:
        copy.wait()

    subs = STEP // 8

    def residuals(step, accs):
        row = pl.multiple_of(step * STEP, STEP)
        region = tile[...]
        chosen = [region == index for index in range(1, NREGION)]
        inner, low, high, lam, most, least = [cell[place] for place in range(6)]
        above, below = [], []
        for index in range(NREGION):
            shift = bins_ref[index] * rows
            up = even[pl.ds(pad + row + shift, STEP), :]
            down = even[pl.ds(pad + row - shift, STEP), :]
            for sub in range(subs):
                at = slice(sub * 8, sub * 8 + 8)
                if index == 0:
                    above.append(up[at])
                    below.append(down[at])
                else:
                    above[sub] = jnp.where(chosen[index - 1], up[at], above[sub])
                    below[sub] = jnp.where(chosen[index - 1], down[at], below[sub])
        own_even = even[pl.ds(pad + row, STEP), :]
        own_odd = odd[pl.ds(row, STEP), :]
        res = [[], []]
        for sub in range(subs):
            at = slice(sub * 8, sub * 8 + 8)
            level = (my_e * ne + step * (STEP // rows) + sub * group).astype(jnp.float32)
            lower = level + low
            upper = level + high
            middle = level + inner
            root_low = jnp.maximum(lower, 0.0) * lax.rsqrt(jnp.maximum(lower, 0.25))
            root_high = jnp.where(upper < NE, upper * lax.rsqrt(upper), 0.0)
            loss = 1.0 + (most * root_low + least * root_high)
            more = loss + lam
            both = 1.0 / (loss * more)
            gain = (least * (middle * lax.rsqrt(middle))) * (3.0 * above[sub] + below[sub])
            new_even = (own_even[at] + gain) * (both * more)
            new_odd = own_odd[at] * (both * loss)
            res[0].append(new_even - own_even[at])
            res[1].append(new_odd - own_odd[at])
            base[0, pl.ds(row + sub * 8, 8), :] = new_even
            base[1, pl.ds(row + sub * 8, 8), :] = new_odd
        new = []
        for field in range(2):
            for index in range(HISTORY + 1):
                value = accs[len(new)]
                if index > 0:
                    other = hg[index - 1, field, pl.ds(row, STEP), :].astype(jnp.float32)
                for sub in range(subs):
                    at = slice(sub * 8, sub * 8 + 8)
                    value = value + res[field][sub] * (other[at] if index > 0 else res[field][sub])
                new.append(value)
        return tuple(new)

    accs = (zero,) * (2 * (HISTORY + 1))
    edge = pad // STEP
    steps = total_rows // STEP
    first_free = jnp.where(has_below_e, edge, 0)
    last_free = jnp.where(has_above_e, steps - edge, steps)
    accs = lax.fori_loop(first_free, last_free, residuals, accs)

    stride = edge // HALO_PIECES
    for index in range(HALO_PIECES):
        @pl.when(has_below_e)
        def _():
            halos[index][0].wait_recv()
            even[pl.ds(index * chunk, chunk), :] = halo[0, index]

        if index == 0:
            continue
        stop = edge if index == HALO_PIECES - 1 else index * stride
        accs = lax.fori_loop(
            jnp.where(has_below_e, (index - 1) * stride, 0),
            jnp.where(has_below_e, stop, 0), residuals, accs,
        )
    for index in range(HALO_PIECES):
        @pl.when(has_above_e)
        def _():
            halos[index][1].wait_recv()
            even[pl.ds(pad + total_rows + index * chunk, chunk), :] = halo[1, index]

        accs = lax.fori_loop(
            jnp.where(has_above_e, steps - edge + index * stride, steps),
            jnp.where(has_above_e, steps - edge + (index + 1) * stride, steps), residuals, accs,
        )

    for position, acc in enumerate(accs):
        at = (position // (HISTORY + 1)) * len(PAIRS) + position % (HISTORY + 1)
        sums[at : at + 1, :] = jnp.sum(acc, axis=0, keepdims=True)
    lane_sum = jnp.sum(sums[...], axis=1, keepdims=True)
    place = lax.broadcasted_iota(jnp.int32, sums.shape, 0) == lax.broadcasted_iota(
        jnp.int32, sums.shape, 1
    )
    row_sum = jnp.sum(jnp.where(place, lane_sum, 0.0), axis=0, keepdims=True)
    part[...] = row_sum
    gathered[me] = row_sum

    def send_sums(step, carry):
        pltpu.make_async_remote_copy(
            part, gathered.at[me], sum_send, sum_recv,
            device_id=device(lax.rem(me + step, count)), device_id_type=MESH,
        ).start()
        return carry

    if paired:
        for index in order:
            pltpu.make_async_remote_copy(
                part, gathered.at[me], sum_send, sum_recv,
                device_id=partner(index), device_id_type=MESH,
            ).start()
    else:
        lax.fori_loop(1, count, send_sums, 0)

    early_sends.append(send_ahead((0,), first_early, last_early, 1))

    for copy in late:
        copy.wait()
    lax.fori_loop(last_early * rows // JOIN, end_early * rows // JOIN, join_history, 0)
    early_sends.append(send_ahead(tuple(range(HISTORY + 1)), last_early, end_early, 2))

    @pl.when(my_s == 0)
    def _():
        lo[...] = jnp.zeros(lo.shape, jnp.float32)
        ahead[0] = jnp.zeros(ahead.shape[1:], jnp.float32)
        mob_lo[...] = jnp.zeros(mob_lo.shape, jnp.float32)

    @pl.when(my_s == n_space - 1)
    def _():
        hi[...] = jnp.zeros(hi.shape, jnp.float32)
        ahead[1] = jnp.zeros(ahead.shape[1:], jnp.float32)
        mob_hi[...] = jnp.zeros(mob_hi.shape, jnp.float32)

    lax.fori_loop(0, cuts[1] // JOIN, join_history, 0)
    lax.fori_loop(end_early * rows // JOIN, total_rows // JOIN, join_history, 0)
    lax.fori_loop(0, total_rows // JOIN, join_current, 0)

    arrive(mobs)

    lanes = lax.broadcasted_iota(jnp.int32, (1, 128), 1)
    column = lanes % COLS
    for row in range(rows):
        mob = mob_ref[row : row + 1, :]
        under = mob_lo[...] if row == 0 else mob_ref[row - 1 : row, :]
        over = mob_hi[...] if row == rows - 1 else mob_ref[row + 1 : row + 2, :]
        w_under = 0.04 * (mob + under)
        w_over = 0.04 * (mob + over)
        if row == 0:
            w_under = jnp.where(has_below, w_under, 0.0)
        if row == rows - 1:
            w_over = jnp.where(has_above, w_over, 0.0)
        w_left = jnp.where(column > 0, 0.04 * (mob + pltpu.roll(mob, 1, 1)), 0.0)
        w_right = jnp.where(column < COLS - 1, 0.04 * (mob + pltpu.roll(mob, 127, 1)), 0.0)
        w_plane = 0.04 * (mob + pltpu.roll(mob, COLS, 1))
        own = 1.0 - (w_under + w_over + w_left + w_right + w_plane)
        weight[0, row] = jnp.broadcast_to(w_under, (8, 128))
        weight[1, row] = jnp.broadcast_to(w_over, (8, 128))
        to = lax.broadcasted_iota(jnp.int32, (128, 128), 1)
        gap = to - lax.broadcasted_iota(jnp.int32, (128, 128), 0)
        matrix = jnp.where(gap == 0, own, 0.0)
        matrix = jnp.where(gap == 1, w_left, matrix)
        matrix = jnp.where(gap == -1, w_right, matrix)
        matrix = jnp.where((gap == COLS) | (gap == -COLS), w_plane, matrix)
        main = matrix.astype(jnp.bfloat16)
        rest = (matrix - main.astype(jnp.float32)).astype(jnp.bfloat16)
        across[row, pl.ds(0, 128), pl.ds(0, 128)] = main
        across[row, pl.ds(128, 128), pl.ds(0, 128)] = main
        across[row, pl.ds(0, 128), pl.ds(128, 128)] = rest
        across[row, pl.ds(128, 128), pl.ds(128, 128)] = jnp.zeros((128, 128), jnp.bfloat16)

    sums_in = gathered.at[pl.ds(0, count - 1)]
    pltpu.make_async_copy(sums_in, sums_in, sum_recv).wait()
    total = jnp.sum(gathered[...], axis=0)
    narrow = [solve(total, field, used_ref) for field in range(2)]

    def mix(which, step, carry):
        at = pl.multiple_of(step * 8, 8)
        for field in range(2):
            for row in which:
                source = pl.ds(at * rows + row, 8, stride=rows)
                value = narrow[field][0] * base[field, source, :]
                for index in range(HISTORY):
                    value = value + narrow[field][index + 1] * hist[index, field, source, :]
                mixed[field, row, pl.ds(at, 8), :] = value
        return carry

    outer = functools.partial(mix, (0, rows - 1))
    level = my_s // 4
    kind = lax.rem(my_s, 4)
    n_up = n_down = jnp.int32(0)
    n_relayed = 0
    if n_space == 4 * len(RELAYS):
        n_relayed = max(RELAYS)
        for index, relayed in enumerate(RELAYS):
            n_down = jnp.where(level == index, relayed, n_down)
            n_up = jnp.where(level == len(RELAYS) - 1 - index, relayed, n_up)

    def relay_copy(source, index, span, target):
        return pltpu.make_async_remote_copy(
            source, passed.at[:, span], relay_send.at[index], relay_recv.at[index],
            device_id=(my_e, target), device_id_type=MESH,
        )

    def by_relay(index):
        if index >= n_relayed:
            return False, False
        return (kind == 3) & (index < n_up), (kind == 0) & (index < n_down)

    def straight(index):
        up_relayed, down_relayed = by_relay(index)
        if index >= n_relayed:
            return has_above, has_below
        return has_above & jnp.logical_not(up_relayed), has_below & jnp.logical_not(down_relayed)

    before, after = lax.rem(my_s + n_space - 3, n_space), lax.rem(my_s + 3, n_space)
    sends = []
    relays = []
    for index, (begin, end) in enumerate(late_spans):
        lax.fori_loop(begin // 8, end // 8, outer, 0)
        span = pl.ds(begin, end - begin)
        copies = pair(
            mixed.at[:, rows - 1, span], lo.at[:, span], mixed.at[:, 0, span], hi.at[:, span],
            [edge_send.at[side, index] for side in range(2)],
            [edge_recv.at[side, index] for side in range(2)],
        )
        sends.append(copies)
        if index < n_relayed:
            relayed = (
                relay_copy(mixed.at[:, rows - 1, span], index, span, before),
                relay_copy(mixed.at[:, 0, span], index, span, after),
            )
            relays.append(relayed)

            @pl.when(by_relay(index)[0])
            def _():
                relayed[0].start()

            @pl.when(by_relay(index)[1])
            def _():
                relayed[1].start()

        @pl.when(straight(index)[0])
        def _():
            copies[0].start()

        @pl.when(straight(index)[1])
        def _():
            copies[1].start()

    lax.fori_loop(first_early // 8, end_early // 8, outer, 0)
    lax.fori_loop(0, ne // 8, functools.partial(mix, tuple(range(1, rows - 1))), 0)

    wide = min(WIDE, ne)

    def drift(block, carry):
        first = pl.multiple_of(block * wide, wide)
        at = pl.ds(first, wide)
        level = (
            (my_e * ne + first).astype(jnp.float32) + 0.5
            + lax.broadcasted_iota(jnp.int32, (wide, 128), 0).astype(jnp.float32)
        ) * (1.0 / NE)
        drive = 0.25 * (level * lax.rsqrt(level))
        for row in range(rows):
            for field in range(2):
                value = mixed[field, row, at, :]
                main = value.astype(jnp.bfloat16)
                rest = (value - main.astype(jnp.float32)).astype(jnp.bfloat16)
                both = jnp.dot(
                    jnp.concatenate([main, rest], axis=1), across[row],
                    preferred_element_type=jnp.float32,
                )
                result = both[:, :128] + both[:, 128:]
                if row > 0:
                    result = result + weight[0, row, 0:1, :] * mixed[field, row - 1, at, :]
                if row < rows - 1:
                    result = result + weight[1, row, 0:1, :] * mixed[field, row + 1, at, :]
                coupled = drive * mixed[1 - field, row, at, :]
                result = result + coupled if field == 0 else result - coupled
                out[field, pl.ds(first * rows + row, wide, stride=rows), :] = result
        return carry

    lax.fori_loop(0, ne // wide, drift, 0)

    onward = []
    for index in range(n_relayed):
        begin, end = late_spans[index]
        span = pl.ds(begin, end - begin)
        up = pltpu.make_async_remote_copy(
            passed.at[:, span], lo.at[:, span], pass_send.at[index], edge_recv.at[0, index],
            device_id=(my_e, lax.rem(my_s + 4, n_space)), device_id_type=MESH,
        )
        down = pltpu.make_async_remote_copy(
            passed.at[:, span], hi.at[:, span], pass_send.at[index], edge_recv.at[1, index],
            device_id=(my_e, lax.rem(my_s + n_space - 4, n_space)), device_id_type=MESH,
        )
        onward.append((up, down))

        @pl.when((kind == 0) & (index < n_up))
        def _():
            relays[index][0].wait_recv()
            up.start()

        @pl.when((kind == 3) & (index < n_down))
        def _():
            relays[index][1].wait_recv()
            down.start()


    def add_edges(step, carry):
        at = pl.multiple_of(step * 8, 8)
        for field in range(2):
            for row, edge_of, kind in ((0, lo, 0), (rows - 1, hi, 1)):
                to = pl.ds(at * rows + row, 8, stride=rows)
                out[field, to, :] = (
                    out[field, to, :] + weight[kind, row] * edge_of[field, pl.ds(at, 8), :]
                )
        return carry

    for copies in early_sends:
        arrive(copies)

    def mix_early(step, carry):
        at = pl.multiple_of(step * 8, 8)
        for side, target in ((0, lo), (1, hi)):
            for field in range(2):
                value = narrow[field][0] * ahead[side, 0, field, pl.ds(at, 8), :]
                for term in range(1, HISTORY + 1):
                    value = value + narrow[field][term] * ahead[side, term, field, pl.ds(at, 8), :]
                target[field, pl.ds(first_early + at, 8), :] = value
        return carry

    lax.fori_loop(0, (end_early - first_early) // 8, mix_early, 0)
    lax.fori_loop(first_early // 8, end_early // 8, add_edges, 0)

    for (begin, end), copies in zip(late_spans, sends):
        arrive(copies)
        lax.fori_loop(begin // 8, end // 8, add_edges, 0)

    sums_out = gathered.at[pl.ds(0, count - 1)]
    pltpu.make_async_copy(sums_out, sums_out, sum_send).wait()

    @pl.when(has_above_e)
    def _():
        for up_e, _ in halos:
            up_e.wait_send()

    @pl.when(has_below_e)
    def _():
        for _, down_e in halos:
            down_e.wait_send()

    for index, copies in enumerate(sends):
        if index < n_relayed:
            @pl.when(by_relay(index)[0])
            def _():
                relays[index][0].wait_send()

            @pl.when(by_relay(index)[1])
            def _():
                relays[index][1].wait_send()

            @pl.when((kind == 0) & (index < n_up))
            def _():
                onward[index][0].wait_send()

            @pl.when((kind == 3) & (index < n_down))
            def _():
                onward[index][1].wait_send()

        @pl.when(straight(index)[0])
        def _():
            copies[0].wait_send()

        @pl.when(straight(index)[1])
        def _():
            copies[1].wait_send()

    sent = [mobs] + early_sends

    @pl.when(has_above)
    def _():
        for up, _ in sent:
            up.wait_send()

    @pl.when(has_below)
    def _():
        for _, down in sent:
            down.wait_send()


def local(n_egrp, n_space, dist, hist_x, hist_g, mobility, region, phonon_bins, coupling, hist_used):
    ne, rows = dist.shape[1], dist.shape[2]
    total = ne * rows
    pad = KMAX * rows
    count = n_egrp * n_space
    early_plan, late_plan = plan(ne)
    early = early_plan[2] - early_plan[0]
    f32 = jnp.float32
    vmem = pl.BlockSpec(memory_space=pltpu.VMEM)
    hbm = pl.BlockSpec(memory_space=pltpu.HBM)
    result = pl.pallas_call(
        functools.partial(kernel, n_egrp, n_space, ne, rows),
        out_shape=jax.ShapeDtypeStruct((2, total, 128), f32),
        in_specs=[hbm] * 8,
        out_specs=vmem,
        scratch_shapes=[
            pltpu.SMEM((NREGION,), jnp.int32),
            pltpu.SMEM((NREGION,), f32),
            pltpu.SMEM((2, HISTORY), jnp.int32),
            pltpu.VMEM((rows, 128), f32),
            pltpu.VMEM((rows, 128), jnp.int32),
            pltpu.VMEM((total + 2 * pad, 128), f32),
            pltpu.VMEM((total, 128), f32),
            pltpu.VMEM((HISTORY, 2, total, 128), jnp.bfloat16),
            pltpu.VMEM((HISTORY, 2, total, 128), jnp.bfloat16),
            pltpu.VMEM((2, total, 128), f32),
            pltpu.VMEM((HISTORY, 2, total, 128), f32),
            pltpu.VMEM((2, rows, ne, 128), f32),
            pltpu.VMEM((2, HISTORY + 1, 2, early, 128), f32),
            pltpu.VMEM((2, ne, 128), f32),
            pltpu.VMEM((2, ne, 128), f32),
            pltpu.VMEM((2, HISTORY + 1, 2, early, 128), f32),
            pltpu.VMEM((6, 8, 128), f32),
            pltpu.VMEM((8, 128), jnp.int32),
            pltpu.VMEM((rows, 256, 256), jnp.bfloat16),
            pltpu.VMEM((2, rows, 8, 128), f32),
            pltpu.VMEM((2, ne, 128), f32),
            pltpu.VMEM((2, 1, 128), f32),
            pltpu.VMEM((1, 128), f32),
            pltpu.VMEM((1, 128), f32),
            pltpu.VMEM((32, 128), f32),
            pltpu.VMEM((1, 128), f32),
            pltpu.VMEM((count, 1, 128), f32),
            pltpu.VMEM((2, HALO_PIECES, pad // HALO_PIECES, 128), f32),
            pltpu.SemaphoreType.DMA((8,)),
            pltpu.SemaphoreType.DMA((5,)),
            pltpu.SemaphoreType.DMA((2, HALO_PIECES)),
            pltpu.SemaphoreType.DMA((2, HALO_PIECES)),
            pltpu.SemaphoreType.DMA((2,)),
            pltpu.SemaphoreType.DMA((2,)),
            pltpu.SemaphoreType.DMA,
            pltpu.SemaphoreType.DMA,
            pltpu.SemaphoreType.DMA((2, len(late_plan))),
            pltpu.SemaphoreType.DMA((2, len(late_plan))),
            pltpu.SemaphoreType.DMA((2, 3)),
            pltpu.SemaphoreType.DMA((2, 3)),
            pltpu.SemaphoreType.DMA((max(RELAYS),)),
            pltpu.SemaphoreType.DMA((max(RELAYS),)),
            pltpu.SemaphoreType.DMA((max(RELAYS),)),
        ],
        compiler_params=pltpu.CompilerParams(
            collective_id=0, has_side_effects=True, vmem_limit_bytes=40 << 20
        ),
    )(
        *[pltpu.with_memory_space_constraint(x, pltpu.HBM) for x in (phonon_bins, coupling, hist_used, mobility, region,
        dist.reshape(2, total, 128),
        hist_x.reshape(HISTORY, 2, total, 128),
        hist_g.reshape(HISTORY, 2, total, 128))],
    )
    return result.reshape(dist.shape)


def solution(mesh):
    in_specs = (
        P(None, "egrp", "space", None),
        P(None, None, "egrp", "space", None),
        P(None, None, "egrp", "space", None),
        P("space", None),
        P("space", None),
        P(),
        P(),
        P(),
    )
    out_specs = P(None, "egrp", "space", None)
    body = functools.partial(local, mesh.shape["egrp"], mesh.shape["space"])
    return jax.shard_map(body, mesh=mesh, in_specs=in_specs, out_specs=out_specs, check_vma=False)
```

```python
import functools
import jax
import jax.numpy as jnp
from jax import lax
from jax.experimental import pallas as pl
from jax.experimental.pallas import tpu as pltpu
from jax.sharding import PartitionSpec as P

NE = 1024
HISTORY = 4
NREGION = 4
KMAX = 64
COLS = 64
PIECES = 16
RELAYS = ((0, 1, 3, 4), (0, 1, 2, 3))
HALO_PIECES = 4
JOIN = 32
STEP = 32
WIDE = 128
PAIRS = [(i, j) for i in range(HISTORY + 1) for j in range(i, HISTORY + 1)]
MESH = pl.DeviceIdType.MESH


def dos_of(energy):
    value = (energy.astype(jnp.float32) + 0.5) * (1.0 / NE)
    return value * lax.rsqrt(value)


def plan(ne):
    piece = ne // PIECES
    ahead = (4 * piece, 4 * piece + max(8, 3 * piece // 16 * 8), 7 * piece)
    odd = [(0, 3), (3, 5), (5, 7), (7, 10), (10, 13), (13, 16)]
    even = [(0, 3), (3, 4), (7, 8), (8, 10), (10, 13), (13, 15), (15, 16)]
    late = [(1, rank, span) for rank, span in enumerate(odd)]
    late += [(0, rank, span) for rank, span in enumerate(even)]
    return ahead, [(field, rank, a * piece, b * piece) for field, rank, (a, b) in late]


def solve(total, field, used_ref):
    def entry(i, j):
        lane = PAIRS.index((min(i, j), max(i, j)))
        return jnp.broadcast_to(total[:, lane : lane + 1], (8, 128))

    size = HISTORY + 1
    valid = [jnp.ones((8, 128), jnp.float32)]
    for index in range(HISTORY):
        valid.append(jnp.full((8, 128), used_ref[field, index].astype(jnp.float32)))
    first = entry(0, 0)
    low = [[None] * size for _ in range(size)]
    scaled = [[None] * size for _ in range(size)]
    inverse = [None] * size
    for j in range(size):
        for i in range(j, size):
            value = valid[i] * valid[j] * entry(i, j)
            if i == j:
                value = value + (1.0 - valid[i]) * first
            for k in range(j):
                value = value - scaled[i][k] * low[j][k]
            scaled[i][j] = value
        inverse[j] = 1.0 / scaled[j][j]
        for i in range(j + 1, size):
            low[i][j] = scaled[i][j] * inverse[j]
    forward = []
    for i in range(size):
        value = valid[i]
        for k in range(i):
            value = value - low[i][k] * forward[k]
        forward.append(value)
    weights = [None] * size
    for i in reversed(range(size)):
        value = forward[i] * inverse[i]
        for k in range(i + 1, size):
            value = value - low[k][i] * weights[k]
        weights[i] = value
    inv_sum = 1.0 / functools.reduce(lambda a, b: a + b, weights)
    return [w * inv_sum for w in weights]


def kernel(
    n_egrp, n_space, ne, rows,
    bins_hbm, coup_hbm, used_hbm, mob_hbm, region_hbm, dist_hbm, hx_hbm, hg_hbm,
    out,
    bins_ref, coup_ref, used_ref, mob_ref, region_ref,
    even, odd, hg, hx, base, ratio, hist, mixed, edges, lo, hi, ahead, cell, tile, across, weight, passed,
    mob_send, mob_lo, mob_hi, sums, part, gathered, halo,
    in_sem, small_sem, halo_send, halo_recv, mob_ssem, mob_rsem, sum_send, sum_recv,
    edge_send, edge_recv, ahead_send, ahead_recv, relay_send, relay_recv, pass_send,
):
    my_e = lax.axis_index("egrp")
    my_s = lax.axis_index("space")
    count = n_egrp * n_space
    me = my_e * n_space + my_s
    total_rows = ne * rows
    pad = KMAX * rows
    group = 8 // rows
    (first_early, mid_early, last_early), late_items = plan(ne)

    def device(index):
        return (index // n_space, lax.rem(index, n_space))

    paired = count <= 64 and n_egrp & (n_egrp - 1) == 0 and n_space & (n_space - 1) == 0
    order = sorted(range(1, count), key=lambda index: -bin(index).count("1")) if paired else []

    def partner(index):
        return (my_e ^ (index // n_space), my_s ^ (index % n_space))

    small = [
        pltpu.make_async_copy(source, target, small_sem.at[index])
        for index, (source, target) in enumerate((
            (region_hbm, region_ref), (bins_hbm, bins_ref), (coup_hbm, coup_ref),
            (mob_hbm, mob_ref), (used_hbm, used_ref),
        ))
    ]
    cuts = [0, first_early * rows, last_early * rows, total_rows]
    parts = [pl.ds(cuts[index], cuts[index + 1] - cuts[index]) for index in range(3)]

    def history_load(source, target, index, sem):
        return pltpu.make_async_copy(
            source.at[:, :, parts[index]], target.at[:, :, parts[index]], in_sem.at[sem]
        )

    first = [history_load(hx_hbm, hx, 1, 2), history_load(hg_hbm, hg, 1, 3)]
    older = [history_load(hg_hbm, hg, 2, 4), history_load(hg_hbm, hg, 0, 5)]
    loads = [
        pltpu.make_async_copy(dist_hbm.at[0], even.at[pl.ds(pad, total_rows)], in_sem.at[0]),
        pltpu.make_async_copy(dist_hbm.at[1], odd, in_sem.at[1]),
    ]
    late = [history_load(hx_hbm, hx, 0, 6), history_load(hx_hbm, hx, 2, 7)]
    barrier = pltpu.get_barrier_semaphore()

    def greet(step, carry):
        pl.semaphore_signal(
            barrier, inc=1, device_id=device(lax.rem(me + step, count)), device_id_type=MESH
        )
        return carry

    if paired:
        for index in [n_space] + [index for index in order if index != n_space]:
            pl.semaphore_signal(barrier, inc=1, device_id=partner(index), device_id_type=MESH)
    else:
        lax.fori_loop(n_space, count, greet, 0)
        lax.fori_loop(1, n_space, greet, 0)
    for copy in small + first + loads[1:] + older + loads[:1] + late:
        copy.start()

    has_below_e = my_e > 0
    has_above_e = my_e < n_egrp - 1
    has_below = my_s > 0
    has_above = my_s < n_space - 1

    for copy in small:
        copy.wait()
    for copy_of in range(group):
        tile[pl.ds(copy_of * rows, rows), :] = region_ref[...]
    mob_send[0] = mob_ref[0:1, :]
    mob_send[1] = mob_ref[rows - 1 : rows, :]

    sums[...] = jnp.zeros(sums.shape, jnp.float32)
    pl.semaphore_wait(barrier, count - 1)

    chunk = pad // HALO_PIECES
    halos = []
    for index in range(HALO_PIECES):
        up_e = pltpu.make_async_remote_copy(
            dist_hbm.at[0, pl.ds(total_rows - pad + index * chunk, chunk)],
            halo.at[0, index],
            halo_send.at[0, index], halo_recv.at[0, index],
            device_id=(lax.rem(my_e + 1, n_egrp), my_s), device_id_type=MESH,
        )
        down_e = pltpu.make_async_remote_copy(
            dist_hbm.at[0, pl.ds(index * chunk, chunk)],
            halo.at[1, index],
            halo_send.at[1, index], halo_recv.at[1, index],
            device_id=(lax.rem(my_e + n_egrp - 1, n_egrp), my_s), device_id_type=MESH,
        )
        halos.append((up_e, down_e))
    next_s = lax.rem(my_s + 1, n_space)
    prev_s = lax.rem(my_s + n_space - 1, n_space)

    def pair(up_source, up_target, down_source, down_target, send, recv):
        return (
            pltpu.make_async_remote_copy(
                up_source, up_target, send[0], recv[0],
                device_id=(my_e, next_s), device_id_type=MESH,
            ),
            pltpu.make_async_remote_copy(
                down_source, down_target, send[1], recv[1],
                device_id=(my_e, prev_s), device_id_type=MESH,
            ),
        )

    def start(copies):
        @pl.when(has_above)
        def _():
            copies[0].start()

        @pl.when(has_below)
        def _():
            copies[1].start()

    def arrive(copies):
        @pl.when(has_below)
        def _():
            copies[0].wait_recv()

        @pl.when(has_above)
        def _():
            copies[1].wait_recv()

    mobs = pair(
        mob_send.at[1], mob_lo, mob_send.at[0], mob_hi,
        [mob_ssem.at[0], mob_ssem.at[1]], [mob_rsem.at[0], mob_rsem.at[1]],
    )

    @pl.when(has_above_e)
    def _():
        for up_e, _ in halos:
            up_e.start()

    @pl.when(has_below_e)
    def _():
        for _, down_e in halos:
            down_e.start()

    start(mobs)

    even[pl.ds(0, pad), :] = jnp.zeros((pad, 128), jnp.float32)
    even[pl.ds(pad + total_rows, pad), :] = jnp.zeros((pad, 128), jnp.float32)

    def join_history(step, carry):
        row = pl.multiple_of(step * JOIN, JOIN)
        for index in range(HISTORY):
            for field in range(2):
                hist[index, field, pl.ds(row, JOIN), :] = hx[
                    index, field, pl.ds(row, JOIN), :
                ].astype(jnp.float32) + 0.5 * hg[index, field, pl.ds(row, JOIN), :].astype(
                    jnp.float32
                )
        return carry

    def pack(terms, step, carry):
        at = pl.multiple_of(step * 8, 8)
        for side, row in ((0, 0), (1, rows - 1)):
            for term in terms:
                source = pl.ds((first_early + at) * rows + row, 8, stride=rows)
                value = base[0, source, :] if term == 0 else hist[term - 1, 0, source, :]
                edges[side, term, pl.ds(at, 8), :] = value
        return carry

    def send_ahead(terms, begin, end, kind):
        at, to = pl.ds(begin - first_early, end - begin), pl.ds(terms[0], len(terms))
        lax.fori_loop(
            (begin - first_early) // 8, (end - first_early) // 8, functools.partial(pack, terms), 0
        )
        copies = pair(
            edges.at[1, to, at], ahead.at[0, to, at],
            edges.at[0, to, at], ahead.at[1, to, at],
            [ahead_send.at[side, kind] for side in range(2)],
            [ahead_recv.at[side, kind] for side in range(2)],
        )
        start(copies)
        return copies

    for copy in first:
        copy.wait()
    lax.fori_loop(cuts[1] // JOIN, cuts[2] // JOIN, join_history, 0)
    terms = tuple(range(1, HISTORY + 1))
    early_sends = [send_ahead(terms, first_early, mid_early, 0)]

    region = tile[...]
    bins = jnp.zeros((8, 128), jnp.int32)
    lam = jnp.zeros((8, 128), jnp.float32)
    for index in range(NREGION):
        bins = jnp.where(region == index, bins_ref[index], bins)
        lam = jnp.where(region == index, coup_ref[index], lam)
    inner = (lax.broadcasted_iota(jnp.int32, (8, 128), 0) // rows).astype(jnp.float32) + 0.5
    reach = bins.astype(jnp.float32)
    for place, value in enumerate((
        inner, inner - reach, inner + reach, lam,
        lam * (1.5 * NE**-0.5), lam * (0.5 * NE**-0.5),
    )):
        cell[place] = value

    subs = STEP // 8
    steps = total_rows // STEP
    edge = pad // STEP
    zero = jnp.zeros((8, 128), jnp.float32)

    def products(field, row, res, accs):
        vectors = [res]
        for index in range(HISTORY):
            value = hg[index, field, pl.ds(row, STEP), :].astype(jnp.float32)
            vectors.append([value[sub * 8 : sub * 8 + 8] for sub in range(subs)])
        new = []
        for position, (i, j) in enumerate(PAIRS):
            value = accs[position]
            for sub in range(subs):
                value = value + vectors[i][sub] * vectors[j][sub]
            new.append(value)
        return tuple(new)

    def level_of(step, sub):
        return (my_e * ne + step * (STEP // rows) + sub * group).astype(jnp.float32)

    def odd_pass(step, accs):
        row = pl.multiple_of(step * STEP, STEP)
        low, high, lam, most, least = [cell[place] for place in range(1, 6)]
        res = []
        for sub in range(subs):
            at = pl.ds(row + sub * 8, 8)
            level = level_of(step, sub)
            lower = level + low
            upper = level + high
            root_low = jnp.maximum(lower, 0.0) * lax.rsqrt(jnp.maximum(lower, 0.25))
            root_high = jnp.where(upper < NE, upper * lax.rsqrt(upper), 0.0)
            loss = 1.0 + (most * root_low + least * root_high)
            more = loss + lam
            both = 1.0 / (loss * more)
            ratio[at, :] = both * more
            own = odd[at, :]
            res.append(own * (both * loss) - own)
            base[1, at, :] = own + 0.5 * res[sub]
        return products(1, row, res, accs)

    def even_pass(step, accs):
        row = pl.multiple_of(step * STEP, STEP)
        region = tile[...]
        chosen = [region == index for index in range(1, NREGION)]
        inner, least = cell[0], cell[5]
        above, below = [], []
        for index in range(NREGION):
            shift = bins_ref[index] * rows
            up = even[pl.ds(pad + row + shift, STEP), :]
            down = even[pl.ds(pad + row - shift, STEP), :]
            for sub in range(subs):
                at = slice(sub * 8, sub * 8 + 8)
                if index == 0:
                    above.append(up[at])
                    below.append(down[at])
                else:
                    above[sub] = jnp.where(chosen[index - 1], up[at], above[sub])
                    below[sub] = jnp.where(chosen[index - 1], down[at], below[sub])
        res = []
        for sub in range(subs):
            at = pl.ds(row + sub * 8, 8)
            middle = level_of(step, sub) + inner
            gain = (least * (middle * lax.rsqrt(middle))) * (3.0 * above[sub] + below[sub])
            own = even[pl.ds(pad + row + sub * 8, 8), :]
            res.append((own + gain) * ratio[at, :] - own)
            base[0, at, :] = own + 0.5 * res[sub]
        return products(0, row, res, accs)

    def share_sums(field, accs):
        for position, acc in enumerate(accs):
            sums[position : position + 1, :] = jnp.sum(acc, axis=0, keepdims=True)
        lane_sum = jnp.sum(sums[...], axis=1, keepdims=True)
        place = lax.broadcasted_iota(jnp.int32, sums.shape, 0) == lax.broadcasted_iota(
            jnp.int32, sums.shape, 1
        )
        row_sum = jnp.sum(jnp.where(place, lane_sum, 0.0), axis=0, keepdims=True)
        part[field] = row_sum
        gathered[field, me] = row_sum

        def send(target):
            pltpu.make_async_remote_copy(
                part.at[field], gathered.at[field, me], sum_send.at[field], sum_recv.at[field],
                device_id=target, device_id_type=MESH,
            ).start()

        def send_step(step, carry):
            send(device(lax.rem(me + step, count)))
            return carry

        if paired:
            for index in order:
                send(partner(index))
        else:
            lax.fori_loop(1, count, send_step, 0)

    def take_sums(field):
        sums_in = gathered.at[field, pl.ds(0, count - 1)]
        pltpu.make_async_copy(sums_in, sums_in, sum_recv.at[field]).wait()
        return solve(jnp.sum(gathered[field], axis=0), field, used_ref)

    for copy in older + loads[1:]:
        copy.wait()
    share_sums(1, lax.fori_loop(0, steps, odd_pass, (zero,) * len(PAIRS)))
    early_sends.append(send_ahead(terms, mid_early, last_early, 1))

    loads[0].wait()
    first_free = jnp.where(has_below_e, edge, 0)
    last_free = jnp.where(has_above_e, steps - edge, steps)
    accs = lax.fori_loop(first_free, last_free, even_pass, (zero,) * len(PAIRS))
    if first_early * rows >= pad and last_early * rows <= total_rows - pad:
        early_sends.append(send_ahead((0,), first_early, last_early, 2))

    stride = edge // HALO_PIECES
    for index in range(HALO_PIECES):
        @pl.when(has_below_e)
        def _():
            halos[index][0].wait_recv()
            even[pl.ds(index * chunk, chunk), :] = halo[0, index]

        if index == 0:
            continue
        stop = edge if index == HALO_PIECES - 1 else index * stride
        accs = lax.fori_loop(
            jnp.where(has_below_e, (index - 1) * stride, 0),
            jnp.where(has_below_e, stop, 0), even_pass, accs,
        )
    for index in range(HALO_PIECES):
        @pl.when(has_above_e)
        def _():
            halos[index][1].wait_recv()
            even[pl.ds(pad + total_rows + index * chunk, chunk), :] = halo[1, index]

        accs = lax.fori_loop(
            jnp.where(has_above_e, steps - edge + index * stride, steps),
            jnp.where(has_above_e, steps - edge + (index + 1) * stride, steps), even_pass, accs,
        )
    share_sums(0, accs)
    if len(early_sends) == 2:
        early_sends.append(send_ahead((0,), first_early, last_early, 2))

    for copy in late:
        copy.wait()
    lax.fori_loop(0, cuts[1] // JOIN, join_history, 0)
    lax.fori_loop(cuts[2] // JOIN, total_rows // JOIN, join_history, 0)

    @pl.when(my_s == 0)
    def _():
        lo[...] = jnp.zeros(lo.shape, jnp.float32)
        ahead[0] = jnp.zeros(ahead.shape[1:], jnp.float32)
        mob_lo[...] = jnp.zeros(mob_lo.shape, jnp.float32)

    @pl.when(my_s == n_space - 1)
    def _():
        hi[...] = jnp.zeros(hi.shape, jnp.float32)
        ahead[1] = jnp.zeros(ahead.shape[1:], jnp.float32)
        mob_hi[...] = jnp.zeros(mob_hi.shape, jnp.float32)

    level = my_s // 4
    kind = lax.rem(my_s, 4)
    ranks = [(jnp.int32(0), jnp.int32(0)), (jnp.int32(0), jnp.int32(0))]
    relaying = n_space == 4 * len(RELAYS[0])
    if relaying:
        for field in range(2):
            n_up, n_down = ranks[field]
            for index, relayed in enumerate(RELAYS[field]):
                n_down = jnp.where(level == index, relayed, n_down)
                n_up = jnp.where(level == len(RELAYS[field]) - 1 - index, relayed, n_up)
            ranks[field] = (n_up, n_down)

    def relayable(field, rank):
        return relaying and rank < max(RELAYS[field])

    def by_relay(field, rank):
        return (kind == 3) & (rank < ranks[field][0]), (kind == 0) & (rank < ranks[field][1])

    def straight(field, rank):
        if not relayable(field, rank):
            return has_above, has_below
        up_relayed, down_relayed = by_relay(field, rank)
        return has_above & jnp.logical_not(up_relayed), has_below & jnp.logical_not(down_relayed)

    before, after = lax.rem(my_s + n_space - 3, n_space), lax.rem(my_s + 3, n_space)

    def remote(source, target, send, recv, space):
        return pltpu.make_async_remote_copy(
            source, target, send, recv, device_id=(my_e, space), device_id_type=MESH
        )

    def mix(field, which, narrow, step, carry):
        at = pl.multiple_of(step * 8, 8)
        for row in which:
            source = pl.ds(at * rows + row, 8, stride=rows)
            value = narrow[0] * base[field, source, :]
            for index in range(HISTORY):
                value = value + narrow[index + 1] * hist[index, field, source, :]
            mixed[field, row, pl.ds(at, 8), :] = value
        return carry

    sends, relays, onward = {}, {}, {}

    def send_late(mine, narrow):
        for index, (field, rank, begin, end) in enumerate(late_items):
            if field != mine:
                continue
            lax.fori_loop(
                begin // 8, end // 8, functools.partial(mix, field, (0, rows - 1), narrow), 0
            )
            span = pl.ds(begin, end - begin)
            copies = pair(
                mixed.at[field, rows - 1, span], lo.at[field, span],
                mixed.at[field, 0, span], hi.at[field, span],
                [edge_send.at[side, index] for side in range(2)],
                [edge_recv.at[side, index] for side in range(2)],
            )
            sends[index] = copies
            if relayable(field, rank):
                relays[index] = [
                    remote(
                        mixed.at[field, row, span], passed.at[field, span], relay_send.at[index],
                        relay_recv.at[index], target,
                    )
                    for row, target in ((rows - 1, before), (0, after))
                ]
                for side in range(2):

                    @pl.when(by_relay(field, rank)[side])
                    def _():
                        relays[index][side].start()

            for side in range(2):

                @pl.when(straight(field, rank)[side])
                def _():
                    copies[side].start()

    def pass_on(mine):
        for index, (field, rank, begin, end) in enumerate(late_items):
            if field != mine or not relayable(field, rank):
                continue
            span = pl.ds(begin, end - begin)
            onward[index] = [
                remote(
                    passed.at[field, span], target.at[field, span], pass_send.at[index],
                    edge_recv.at[side, index], lax.rem(my_s + n_space + jump, n_space),
                )
                for side, target, jump in ((0, lo, 4), (1, hi, -4))
            ]
            for side, own_kind in ((0, 0), (1, 3)):

                @pl.when((kind == own_kind) & (rank < ranks[field][side]))
                def _():
                    relays[index][side].wait_recv()
                    onward[index][side].start()

    middle_rows = tuple(range(1, rows - 1))
    odd_c = take_sums(1)
    send_late(1, odd_c)
    lax.fori_loop(0, ne // 8, functools.partial(mix, 1, middle_rows, odd_c), 0)

    arrive(mobs)

    lanes = lax.broadcasted_iota(jnp.int32, (1, 128), 1)
    column = lanes % COLS
    for row in range(rows):
        mob = mob_ref[row : row + 1, :]
        under = mob_lo[...] if row == 0 else mob_ref[row - 1 : row, :]
        over = mob_hi[...] if row == rows - 1 else mob_ref[row + 1 : row + 2, :]
        w_under = 0.04 * (mob + under)
        w_over = 0.04 * (mob + over)
        if row == 0:
            w_under = jnp.where(has_below, w_under, 0.0)
        if row == rows - 1:
            w_over = jnp.where(has_above, w_over, 0.0)
        w_left = jnp.where(column > 0, 0.04 * (mob + pltpu.roll(mob, 1, 1)), 0.0)
        w_right = jnp.where(column < COLS - 1, 0.04 * (mob + pltpu.roll(mob, 127, 1)), 0.0)
        w_plane = 0.04 * (mob + pltpu.roll(mob, COLS, 1))
        own = 1.0 - (w_under + w_over + w_left + w_right + w_plane)
        weight[0, row] = jnp.broadcast_to(w_under, (8, 128))
        weight[1, row] = jnp.broadcast_to(w_over, (8, 128))
        to = lax.broadcasted_iota(jnp.int32, (128, 128), 1)
        gap = to - lax.broadcasted_iota(jnp.int32, (128, 128), 0)
        matrix = jnp.where(gap == 0, own, 0.0)
        matrix = jnp.where(gap == 1, w_left, matrix)
        matrix = jnp.where(gap == -1, w_right, matrix)
        matrix = jnp.where((gap == COLS) | (gap == -COLS), w_plane, matrix)
        main = matrix.astype(jnp.bfloat16)
        rest = (matrix - main.astype(jnp.float32)).astype(jnp.bfloat16)
        across[row, pl.ds(0, 128), pl.ds(0, 128)] = main
        across[row, pl.ds(128, 128), pl.ds(0, 128)] = main
        across[row, pl.ds(0, 128), pl.ds(128, 128)] = rest
        across[row, pl.ds(128, 128), pl.ds(128, 128)] = jnp.zeros((128, 128), jnp.bfloat16)

    even_c = take_sums(0)
    send_late(0, even_c)
    pass_on(1)
    lax.fori_loop(
        first_early // 8, last_early // 8, functools.partial(mix, 0, (0, rows - 1), even_c), 0
    )
    lax.fori_loop(0, ne // 8, functools.partial(mix, 0, middle_rows, even_c), 0)

    wide = min(WIDE, ne)

    def drift(block, carry):
        first = pl.multiple_of(block * wide, wide)
        at = pl.ds(first, wide)
        level = (
            (my_e * ne + first).astype(jnp.float32) + 0.5
            + lax.broadcasted_iota(jnp.int32, (wide, 128), 0).astype(jnp.float32)
        ) * (1.0 / NE)
        drive = 0.25 * (level * lax.rsqrt(level))
        for row in range(rows):
            for field in range(2):
                value = mixed[field, row, at, :]
                main = value.astype(jnp.bfloat16)
                rest = (value - main.astype(jnp.float32)).astype(jnp.bfloat16)
                both = jnp.dot(
                    jnp.concatenate([main, rest], axis=1), across[row],
                    preferred_element_type=jnp.float32,
                )
                result = both[:, :128] + both[:, 128:]
                if row > 0:
                    result = result + weight[0, row, 0:1, :] * mixed[field, row - 1, at, :]
                if row < rows - 1:
                    result = result + weight[1, row, 0:1, :] * mixed[field, row + 1, at, :]
                coupled = drive * mixed[1 - field, row, at, :]
                result = result + coupled if field == 0 else result - coupled
                out[field, pl.ds(first * rows + row, wide, stride=rows), :] = result
        return carry

    lax.fori_loop(0, ne // wide, drift, 0)

    pass_on(0)

    def add_edges(field, step, carry):
        at = pl.multiple_of(step * 8, 8)
        for row, edge_of, side in ((0, lo, 0), (rows - 1, hi, 1)):
            to = pl.ds(at * rows + row, 8, stride=rows)
            out[field, to, :] = (
                out[field, to, :] + weight[side, row] * edge_of[field, pl.ds(at, 8), :]
            )
        return carry

    for copies in early_sends:
        arrive(copies)

    def mix_early(step, carry):
        at = pl.multiple_of(step * 8, 8)
        for side, target in ((0, lo), (1, hi)):
            value = even_c[0] * ahead[side, 0, pl.ds(at, 8), :]
            for term in range(1, HISTORY + 1):
                value = value + even_c[term] * ahead[side, term, pl.ds(at, 8), :]
            target[0, pl.ds(first_early + at, 8), :] = value
        return carry

    lax.fori_loop(0, (last_early - first_early) // 8, mix_early, 0)
    lax.fori_loop(first_early // 8, last_early // 8, functools.partial(add_edges, 0), 0)

    for index, (field, rank, begin, end) in enumerate(late_items):
        arrive(sends[index])
        lax.fori_loop(begin // 8, end // 8, functools.partial(add_edges, field), 0)

    for field in range(2):
        sums_out = gathered.at[field, pl.ds(0, count - 1)]
        pltpu.make_async_copy(sums_out, sums_out, sum_send.at[field]).wait()

    @pl.when(has_above_e)
    def _():
        for up_e, _ in halos:
            up_e.wait_send()

    @pl.when(has_below_e)
    def _():
        for _, down_e in halos:
            down_e.wait_send()

    for index, (field, rank, begin, end) in enumerate(late_items):
        for side, own_kind in ((0, 0), (1, 3)):
            if relayable(field, rank):

                @pl.when(by_relay(field, rank)[side])
                def _():
                    relays[index][side].wait_send()

                @pl.when((kind == own_kind) & (rank < ranks[field][side]))
                def _():
                    onward[index][side].wait_send()

            @pl.when(straight(field, rank)[side])
            def _():
                sends[index][side].wait_send()

    sent = [mobs] + early_sends

    @pl.when(has_above)
    def _():
        for up, _ in sent:
            up.wait_send()

    @pl.when(has_below)
    def _():
        for _, down in sent:
            down.wait_send()


def local(n_egrp, n_space, dist, hist_x, hist_g, mobility, region, phonon_bins, coupling, hist_used):
    ne, rows = dist.shape[1], dist.shape[2]
    total = ne * rows
    pad = KMAX * rows
    count = n_egrp * n_space
    early_plan, late_plan = plan(ne)
    early = early_plan[2] - early_plan[0]
    f32 = jnp.float32
    vmem = pl.BlockSpec(memory_space=pltpu.VMEM)
    hbm = pl.BlockSpec(memory_space=pltpu.HBM)
    result = pl.pallas_call(
        functools.partial(kernel, n_egrp, n_space, ne, rows),
        out_shape=jax.ShapeDtypeStruct((2, total, 128), f32),
        in_specs=[hbm] * 8,
        out_specs=vmem,
        scratch_shapes=[
            pltpu.SMEM((NREGION,), jnp.int32),
            pltpu.SMEM((NREGION,), f32),
            pltpu.SMEM((2, HISTORY), jnp.int32),
            pltpu.VMEM((rows, 128), f32),
            pltpu.VMEM((rows, 128), jnp.int32),
            pltpu.VMEM((total + 2 * pad, 128), f32),
            pltpu.VMEM((total, 128), f32),
            pltpu.VMEM((HISTORY, 2, total, 128), jnp.bfloat16),
            pltpu.VMEM((HISTORY, 2, total, 128), jnp.bfloat16),
            pltpu.VMEM((2, total, 128), f32),
            pltpu.VMEM((total, 128), f32),
            pltpu.VMEM((HISTORY, 2, total, 128), f32),
            pltpu.VMEM((2, rows, ne, 128), f32),
            pltpu.VMEM((2, HISTORY + 1, early, 128), f32),
            pltpu.VMEM((2, ne, 128), f32),
            pltpu.VMEM((2, ne, 128), f32),
            pltpu.VMEM((2, HISTORY + 1, early, 128), f32),
            pltpu.VMEM((6, 8, 128), f32),
            pltpu.VMEM((8, 128), jnp.int32),
            pltpu.VMEM((rows, 256, 256), jnp.bfloat16),
            pltpu.VMEM((2, rows, 8, 128), f32),
            pltpu.VMEM((2, ne, 128), f32),
            pltpu.VMEM((2, 1, 128), f32),
            pltpu.VMEM((1, 128), f32),
            pltpu.VMEM((1, 128), f32),
            pltpu.VMEM((16, 128), f32),
            pltpu.VMEM((2, 1, 128), f32),
            pltpu.VMEM((2, count, 1, 128), f32),
            pltpu.VMEM((2, HALO_PIECES, pad // HALO_PIECES, 128), f32),
            pltpu.SemaphoreType.DMA((8,)),
            pltpu.SemaphoreType.DMA((5,)),
            pltpu.SemaphoreType.DMA((2, HALO_PIECES)),
            pltpu.SemaphoreType.DMA((2, HALO_PIECES)),
            pltpu.SemaphoreType.DMA((2,)),
            pltpu.SemaphoreType.DMA((2,)),
            pltpu.SemaphoreType.DMA((2,)),
            pltpu.SemaphoreType.DMA((2,)),
            pltpu.SemaphoreType.DMA((2, len(late_plan))),
            pltpu.SemaphoreType.DMA((2, len(late_plan))),
            pltpu.SemaphoreType.DMA((2, 3)),
            pltpu.SemaphoreType.DMA((2, 3)),
            pltpu.SemaphoreType.DMA((len(late_plan),)),
            pltpu.SemaphoreType.DMA((len(late_plan),)),
            pltpu.SemaphoreType.DMA((len(late_plan),)),
        ],
        compiler_params=pltpu.CompilerParams(
            collective_id=0, has_side_effects=True, vmem_limit_bytes=40 << 20
        ),
    )(
        *[pltpu.with_memory_space_constraint(x, pltpu.HBM) for x in (phonon_bins, coupling, hist_used, mobility, region,
        dist.reshape(2, total, 128),
        hist_x.reshape(HISTORY, 2, total, 128),
        hist_g.reshape(HISTORY, 2, total, 128))],
    )
    return result.reshape(dist.shape)


def solution(mesh):
    in_specs = (
        P(None, "egrp", "space", None),
        P(None, None, "egrp", "space", None),
        P(None, None, "egrp", "space", None),
        P("space", None),
        P("space", None),
        P(),
        P(),
        P(),
    )
    out_specs = P(None, "egrp", "space", None)
    body = functools.partial(local, mesh.shape["egrp"], mesh.shape["space"])
    return jax.shard_map(body, mesh=mesh, in_specs=in_specs, out_specs=out_specs, check_vma=False)
```

```python
import functools
import jax
import jax.numpy as jnp
from jax import lax
from jax.experimental import pallas as pl
from jax.experimental.pallas import tpu as pltpu
from jax.sharding import PartitionSpec as P

NE = 1024
HISTORY = 4
NREGION = 4
KMAX = 64
COLS = 64
PIECES = 16
RELAYS = ((0, 1, 3, 4), (0, 1, 2, 3))
HALO_PIECES = 4
JOIN = 32
STEP = 64
WIDE = 128
PAIRS = [(i, j) for i in range(HISTORY + 1) for j in range(i, HISTORY + 1)]
MESH = pl.DeviceIdType.MESH


def dos_of(energy):
    value = (energy.astype(jnp.float32) + 0.5) * (1.0 / NE)
    return value * lax.rsqrt(value)


def plan(ne):
    piece = ne // PIECES
    ahead = (4 * piece, 5 * piece, 7 * piece)
    odd = [(0, 3), (3, 5), (5, 7), (7, 10), (10, 13), (13, 16)]
    even = [(0, 3), (3, 4), (7, 8), (8, 10), (10, 13), (13, 15), (15, 16)]
    late = [(1, rank, span) for rank, span in enumerate(odd)]
    late += [(0, rank, span) for rank, span in enumerate(even)]
    return ahead, [(field, rank, a * piece, b * piece) for field, rank, (a, b) in late]


def solve(total, field, used_ref):
    def entry(i, j):
        lane = PAIRS.index((min(i, j), max(i, j)))
        return jnp.broadcast_to(total[:, lane : lane + 1], (8, 128))

    size = HISTORY + 1
    valid = [jnp.ones((8, 128), jnp.float32)]
    for index in range(HISTORY):
        valid.append(jnp.full((8, 128), used_ref[field, index].astype(jnp.float32)))
    first = entry(0, 0)
    low = [[None] * size for _ in range(size)]
    scaled = [[None] * size for _ in range(size)]
    inverse = [None] * size
    for j in range(size):
        for i in range(j, size):
            value = valid[i] * valid[j] * entry(i, j)
            if i == j:
                value = value + (1.0 - valid[i]) * first
            for k in range(j):
                value = value - scaled[i][k] * low[j][k]
            scaled[i][j] = value
        inverse[j] = 1.0 / scaled[j][j]
        for i in range(j + 1, size):
            low[i][j] = scaled[i][j] * inverse[j]
    forward = []
    for i in range(size):
        value = valid[i]
        for k in range(i):
            value = value - low[i][k] * forward[k]
        forward.append(value)
    weights = [None] * size
    for i in reversed(range(size)):
        value = forward[i] * inverse[i]
        for k in range(i + 1, size):
            value = value - low[k][i] * weights[k]
        weights[i] = value
    inv_sum = 1.0 / functools.reduce(lambda a, b: a + b, weights)
    return [w * inv_sum for w in weights]


def kernel(
    n_egrp, n_space, ne, rows,
    bins_hbm, coup_hbm, used_hbm, mob_hbm, region_hbm, dist_hbm, hx_hbm, hg_hbm,
    out,
    bins_ref, coup_ref, used_ref, mob_ref, region_ref,
    even, odd, hg, hx, base, ratio, hist, mixed, edges, lo, hi, ahead, cell, tile, across, weight, passed,
    mob_send, mob_lo, mob_hi, sums, part, gathered, halo,
    in_sem, small_sem, halo_send, halo_recv, mob_ssem, mob_rsem, sum_send, sum_recv,
    edge_send, edge_recv, ahead_send, ahead_recv, relay_send, relay_recv, pass_send,
):
    my_e = lax.axis_index("egrp")
    my_s = lax.axis_index("space")
    count = n_egrp * n_space
    me = my_e * n_space + my_s
    total_rows = ne * rows
    pad = KMAX * rows
    group = 8 // rows
    (first_early, mid_early, last_early), late_items = plan(ne)

    def device(index):
        return (index // n_space, lax.rem(index, n_space))

    paired = count <= 64 and n_egrp & (n_egrp - 1) == 0 and n_space & (n_space - 1) == 0
    order = sorted(range(1, count), key=lambda index: -bin(index).count("1")) if paired else []

    def partner(index):
        return (my_e ^ (index // n_space), my_s ^ (index % n_space))

    small = [
        pltpu.make_async_copy(source, target, small_sem.at[index])
        for index, (source, target) in enumerate((
            (region_hbm, region_ref), (bins_hbm, bins_ref), (coup_hbm, coup_ref),
            (mob_hbm, mob_ref), (used_hbm, used_ref),
        ))
    ]
    cuts = [0, first_early * rows, last_early * rows, total_rows]
    parts = [pl.ds(cuts[index], cuts[index + 1] - cuts[index]) for index in range(3)]

    def history_load(source, target, field, rows_in, sem):
        return pltpu.make_async_copy(
            source.at[:, field, rows_in], target.at[:, field, rows_in], in_sem.at[sem]
        )

    whole = pl.ds(0, total_rows)
    first = [history_load(hx_hbm, hx, 0, parts[1], 0), history_load(hg_hbm, hg, 0, parts[1], 1)]
    odd_loads = [
        pltpu.make_async_copy(dist_hbm.at[1], odd, in_sem.at[2]),
        history_load(hg_hbm, hg, 1, whole, 3),
    ]
    even_loads = [
        pltpu.make_async_copy(dist_hbm.at[0], even.at[pl.ds(pad, total_rows)], in_sem.at[4]),
        history_load(hg_hbm, hg, 0, parts[0], 5), history_load(hg_hbm, hg, 0, parts[2], 6),
    ]
    late = [
        history_load(hx_hbm, hx, 1, whole, 7), history_load(hx_hbm, hx, 0, parts[0], 8),
        history_load(hx_hbm, hx, 0, parts[2], 9),
    ]

    barrier = pltpu.get_barrier_semaphore()

    def greet(step, carry):
        pl.semaphore_signal(
            barrier, inc=1, device_id=device(lax.rem(me + step, count)), device_id_type=MESH
        )
        return carry

    if paired:
        for index in [n_space] + [index for index in order if index != n_space]:
            pl.semaphore_signal(barrier, inc=1, device_id=partner(index), device_id_type=MESH)
    else:
        lax.fori_loop(n_space, count, greet, 0)
        lax.fori_loop(1, n_space, greet, 0)
    for copy in small + first + odd_loads + even_loads + late:
        copy.start()

    has_below_e = my_e > 0
    has_above_e = my_e < n_egrp - 1
    has_below = my_s > 0
    has_above = my_s < n_space - 1

    for copy in small:
        copy.wait()
    for copy_of in range(group):
        tile[pl.ds(copy_of * rows, rows), :] = region_ref[...]
    mob_send[0] = mob_ref[0:1, :]
    mob_send[1] = mob_ref[rows - 1 : rows, :]

    sums[...] = jnp.zeros(sums.shape, jnp.float32)
    pl.semaphore_wait(barrier, count - 1)

    chunk = pad // HALO_PIECES
    halos = []
    for index in range(HALO_PIECES):
        up_e = pltpu.make_async_remote_copy(
            dist_hbm.at[0, pl.ds(total_rows - pad + index * chunk, chunk)],
            halo.at[0, index],
            halo_send.at[0, index], halo_recv.at[0, index],
            device_id=(lax.rem(my_e + 1, n_egrp), my_s), device_id_type=MESH,
        )
        down_e = pltpu.make_async_remote_copy(
            dist_hbm.at[0, pl.ds(index * chunk, chunk)],
            halo.at[1, index],
            halo_send.at[1, index], halo_recv.at[1, index],
            device_id=(lax.rem(my_e + n_egrp - 1, n_egrp), my_s), device_id_type=MESH,
        )
        halos.append((up_e, down_e))
    next_s = lax.rem(my_s + 1, n_space)
    prev_s = lax.rem(my_s + n_space - 1, n_space)

    def pair(up_source, up_target, down_source, down_target, send, recv):
        return (
            pltpu.make_async_remote_copy(
                up_source, up_target, send[0], recv[0],
                device_id=(my_e, next_s), device_id_type=MESH,
            ),
            pltpu.make_async_remote_copy(
                down_source, down_target, send[1], recv[1],
                device_id=(my_e, prev_s), device_id_type=MESH,
            ),
        )

    def start(copies):
        @pl.when(has_above)
        def _():
            copies[0].start()

        @pl.when(has_below)
        def _():
            copies[1].start()

    def arrive(copies):
        @pl.when(has_below)
        def _():
            copies[0].wait_recv()

        @pl.when(has_above)
        def _():
            copies[1].wait_recv()

    mobs = pair(
        mob_send.at[1], mob_lo, mob_send.at[0], mob_hi,
        [mob_ssem.at[0], mob_ssem.at[1]], [mob_rsem.at[0], mob_rsem.at[1]],
    )

    @pl.when(has_above_e)
    def _():
        for up_e, _ in halos:
            up_e.start()

    @pl.when(has_below_e)
    def _():
        for _, down_e in halos:
            down_e.start()

    start(mobs)

    even[pl.ds(0, pad), :] = jnp.zeros((pad, 128), jnp.float32)
    even[pl.ds(pad + total_rows, pad), :] = jnp.zeros((pad, 128), jnp.float32)

    def join_history(field, step, carry):
        at = pl.ds(pl.multiple_of(step * JOIN, JOIN), JOIN)
        for index in range(HISTORY):
            hist[index, field, at, :] = hx[index, field, at, :].astype(jnp.float32) + 0.5 * hg[
                index, field, at, :
            ].astype(jnp.float32)
        return carry

    join_even, join_odd = [functools.partial(join_history, field) for field in range(2)]

    def pack(terms, step, carry):
        at = pl.multiple_of(step * 8, 8)
        for side, row in ((0, 0), (1, rows - 1)):
            for term in terms:
                source = pl.ds((first_early + at) * rows + row, 8, stride=rows)
                value = base[0, source, :] if term == 0 else hist[term - 1, 0, source, :]
                edges[side, term, pl.ds(at, 8), :] = value
        return carry

    def send_ahead(terms, begin, end, kind):
        at, to = pl.ds(begin - first_early, end - begin), pl.ds(terms[0], len(terms))
        lax.fori_loop(
            (begin - first_early) // 8, (end - first_early) // 8, functools.partial(pack, terms), 0
        )
        copies = pair(
            edges.at[1, to, at], ahead.at[0, to, at],
            edges.at[0, to, at], ahead.at[1, to, at],
            [ahead_send.at[side, kind] for side in range(2)],
            [ahead_recv.at[side, kind] for side in range(2)],
        )
        start(copies)
        return copies

    for copy in first:
        copy.wait()
    lax.fori_loop(cuts[1] // JOIN, cuts[2] // JOIN, join_even, 0)
    terms = tuple(range(1, HISTORY + 1))
    early_sends = [send_ahead(terms, first_early, mid_early, 0)]

    region = tile[...]
    bins = jnp.zeros((8, 128), jnp.int32)
    lam = jnp.zeros((8, 128), jnp.float32)
    for index in range(NREGION):
        bins = jnp.where(region == index, bins_ref[index], bins)
        lam = jnp.where(region == index, coup_ref[index], lam)
    inner = (lax.broadcasted_iota(jnp.int32, (8, 128), 0) // rows).astype(jnp.float32) + 0.5
    reach = bins.astype(jnp.float32)
    for place, value in enumerate((
        inner, inner - reach, inner + reach, lam,
        lam * (1.5 * NE**-0.5), lam * (0.5 * NE**-0.5),
    )):
        cell[place] = value

    subs = STEP // 8
    steps = total_rows // STEP
    edge = pad // STEP
    zero = jnp.zeros((8, 128), jnp.float32)

    def products(field, row, res, accs):
        vectors = [res]
        for index in range(HISTORY):
            value = hg[index, field, pl.ds(row, STEP), :].astype(jnp.float32)
            vectors.append([value[sub * 8 : sub * 8 + 8] for sub in range(subs)])
        new = []
        for position, (i, j) in enumerate(PAIRS):
            value = accs[position]
            for sub in range(subs):
                value = value + vectors[i][sub] * vectors[j][sub]
            new.append(value)
        return tuple(new)

    def level_of(step, sub):
        return (my_e * ne + step * (STEP // rows) + sub * group).astype(jnp.float32)

    def odd_pass(step, accs):
        row = pl.multiple_of(step * STEP, STEP)
        low, high, lam, most, least = [cell[place] for place in range(1, 6)]
        res = []
        for sub in range(subs):
            at = pl.ds(row + sub * 8, 8)
            level = level_of(step, sub)
            lower = level + low
            upper = level + high
            root_low = jnp.maximum(lower, 0.0) * lax.rsqrt(jnp.maximum(lower, 0.25))
            root_high = jnp.where(upper < NE, upper * lax.rsqrt(upper), 0.0)
            loss = 1.0 + (most * root_low + least * root_high)
            more = loss + lam
            both = 1.0 / (loss * more)
            ratio[at, :] = both * more
            own = odd[at, :]
            res.append(own * (both * loss) - own)
            base[1, at, :] = own + 0.5 * res[sub]
        return products(1, row, res, accs)

    def even_pass(step, accs):
        row = pl.multiple_of(step * STEP, STEP)
        region = tile[...]
        chosen = [region == index for index in range(1, NREGION)]
        inner, least = cell[0], cell[5]
        above, below = [], []
        for index in range(NREGION):
            shift = bins_ref[index] * rows
            up = even[pl.ds(pad + row + shift, STEP), :]
            down = even[pl.ds(pad + row - shift, STEP), :]
            for sub in range(subs):
                at = slice(sub * 8, sub * 8 + 8)
                if index == 0:
                    above.append(up[at])
                    below.append(down[at])
                else:
                    above[sub] = jnp.where(chosen[index - 1], up[at], above[sub])
                    below[sub] = jnp.where(chosen[index - 1], down[at], below[sub])
        res = []
        for sub in range(subs):
            at = pl.ds(row + sub * 8, 8)
            middle = level_of(step, sub) + inner
            gain = (least * (middle * lax.rsqrt(middle))) * (3.0 * above[sub] + below[sub])
            own = even[pl.ds(pad + row + sub * 8, 8), :]
            res.append((own + gain) * ratio[at, :] - own)
            base[0, at, :] = own + 0.5 * res[sub]
        return products(0, row, res, accs)

    def share_sums(field, accs):
        for position, acc in enumerate(accs):
            sums[position : position + 1, :] = jnp.sum(acc, axis=0, keepdims=True)
        lane_sum = jnp.sum(sums[...], axis=1, keepdims=True)
        place = lax.broadcasted_iota(jnp.int32, sums.shape, 0) == lax.broadcasted_iota(
            jnp.int32, sums.shape, 1
        )
        row_sum = jnp.sum(jnp.where(place, lane_sum, 0.0), axis=0, keepdims=True)
        part[field] = row_sum
        gathered[field, me] = row_sum

        def send(target):
            pltpu.make_async_remote_copy(
                part.at[field], gathered.at[field, me], sum_send.at[field], sum_recv.at[field],
                device_id=target, device_id_type=MESH,
            ).start()

        def send_step(step, carry):
            send(device(lax.rem(me + step, count)))
            return carry

        if paired:
            for index in order:
                send(partner(index))
        else:
            lax.fori_loop(1, count, send_step, 0)

    def take_sums(field):
        sums_in = gathered.at[field, pl.ds(0, count - 1)]
        pltpu.make_async_copy(sums_in, sums_in, sum_recv.at[field]).wait()
        return solve(jnp.sum(gathered[field], axis=0), field, used_ref)

    for copy in odd_loads:
        copy.wait()
    share_sums(1, lax.fori_loop(0, steps, odd_pass, (zero,) * len(PAIRS)))
    early_sends.append(send_ahead(terms, mid_early, last_early, 1))

    for copy in even_loads:
        copy.wait()
    first_free = jnp.where(has_below_e, edge, 0)
    last_free = jnp.where(has_above_e, steps - edge, steps)
    accs = lax.fori_loop(first_free, last_free, even_pass, (zero,) * len(PAIRS))
    if first_early * rows >= pad and last_early * rows <= total_rows - pad:
        early_sends.append(send_ahead((0,), first_early, last_early, 2))

    stride = edge // HALO_PIECES
    for index in range(HALO_PIECES):
        @pl.when(has_below_e)
        def _():
            halos[index][0].wait_recv()
            even[pl.ds(index * chunk, chunk), :] = halo[0, index]

        if index == 0:
            continue
        stop = edge if index == HALO_PIECES - 1 else index * stride
        accs = lax.fori_loop(
            jnp.where(has_below_e, (index - 1) * stride, 0),
            jnp.where(has_below_e, stop, 0), even_pass, accs,
        )
    for index in range(HALO_PIECES):
        @pl.when(has_above_e)
        def _():
            halos[index][1].wait_recv()
            even[pl.ds(pad + total_rows + index * chunk, chunk), :] = halo[1, index]

        accs = lax.fori_loop(
            jnp.where(has_above_e, steps - edge + index * stride, steps),
            jnp.where(has_above_e, steps - edge + (index + 1) * stride, steps), even_pass, accs,
        )
    share_sums(0, accs)
    if len(early_sends) == 2:
        early_sends.append(send_ahead((0,), first_early, last_early, 2))

    for copy in late:
        copy.wait()
    lax.fori_loop(0, total_rows // JOIN, join_odd, 0)

    @pl.when(my_s == 0)
    def _():
        lo[...] = jnp.zeros(lo.shape, jnp.float32)
        ahead[0] = jnp.zeros(ahead.shape[1:], jnp.float32)
        mob_lo[...] = jnp.zeros(mob_lo.shape, jnp.float32)

    @pl.when(my_s == n_space - 1)
    def _():
        hi[...] = jnp.zeros(hi.shape, jnp.float32)
        ahead[1] = jnp.zeros(ahead.shape[1:], jnp.float32)
        mob_hi[...] = jnp.zeros(mob_hi.shape, jnp.float32)

    level = my_s // 4
    kind = lax.rem(my_s, 4)
    ranks = [(jnp.int32(0), jnp.int32(0)), (jnp.int32(0), jnp.int32(0))]
    relaying = n_space == 4 * len(RELAYS[0])
    if relaying:
        for field in range(2):
            n_up, n_down = ranks[field]
            for index, relayed in enumerate(RELAYS[field]):
                n_down = jnp.where(level == index, relayed, n_down)
                n_up = jnp.where(level == len(RELAYS[field]) - 1 - index, relayed, n_up)
            ranks[field] = (n_up, n_down)

    def relayable(field, rank):
        return relaying and rank < max(RELAYS[field])

    def by_relay(field, rank):
        return (kind == 3) & (rank < ranks[field][0]), (kind == 0) & (rank < ranks[field][1])

    def straight(field, rank):
        if not relayable(field, rank):
            return has_above, has_below
        up_relayed, down_relayed = by_relay(field, rank)
        return has_above & jnp.logical_not(up_relayed), has_below & jnp.logical_not(down_relayed)

    before, after = lax.rem(my_s + n_space - 3, n_space), lax.rem(my_s + 3, n_space)

    def remote(source, target, send, recv, space):
        return pltpu.make_async_remote_copy(
            source, target, send, recv, device_id=(my_e, space), device_id_type=MESH
        )

    def mix(field, which, narrow, step, carry):
        at = pl.multiple_of(step * 8, 8)
        for row in which:
            source = pl.ds(at * rows + row, 8, stride=rows)
            value = narrow[0] * base[field, source, :]
            for index in range(HISTORY):
                value = value + narrow[index + 1] * hist[index, field, source, :]
            mixed[field, row, pl.ds(at, 8), :] = value
        return carry

    sends, relays, onward = {}, {}, {}

    def send_late(mine, narrow):
        for index, (field, rank, begin, end) in enumerate(late_items):
            if field != mine:
                continue
            lax.fori_loop(
                begin // 8, end // 8, functools.partial(mix, field, (0, rows - 1), narrow), 0
            )
            span = pl.ds(begin, end - begin)
            copies = pair(
                mixed.at[field, rows - 1, span], lo.at[field, span],
                mixed.at[field, 0, span], hi.at[field, span],
                [edge_send.at[side, index] for side in range(2)],
                [edge_recv.at[side, index] for side in range(2)],
            )
            sends[index] = copies
            if relayable(field, rank):
                relays[index] = [
                    remote(
                        mixed.at[field, row, span], passed.at[field, span], relay_send.at[index],
                        relay_recv.at[index], target,
                    )
                    for row, target in ((rows - 1, before), (0, after))
                ]
                for side in range(2):

                    @pl.when(by_relay(field, rank)[side])
                    def _():
                        relays[index][side].start()

            for side in range(2):

                @pl.when(straight(field, rank)[side])
                def _():
                    copies[side].start()

    def pass_on(mine):
        for index, (field, rank, begin, end) in enumerate(late_items):
            if field != mine or not relayable(field, rank):
                continue
            span = pl.ds(begin, end - begin)
            onward[index] = [
                remote(
                    passed.at[field, span], target.at[field, span], pass_send.at[index],
                    edge_recv.at[side, index], lax.rem(my_s + n_space + jump, n_space),
                )
                for side, target, jump in ((0, lo, 4), (1, hi, -4))
            ]
            for side, own_kind in ((0, 0), (1, 3)):

                @pl.when((kind == own_kind) & (rank < ranks[field][side]))
                def _():
                    relays[index][side].wait_recv()
                    onward[index][side].start()

    middle_rows = tuple(range(1, rows - 1))
    odd_c = take_sums(1)
    send_late(1, odd_c)
    lax.fori_loop(0, ne // 8, functools.partial(mix, 1, middle_rows, odd_c), 0)

    arrive(mobs)

    lanes = lax.broadcasted_iota(jnp.int32, (1, 128), 1)
    column = lanes % COLS
    for row in range(rows):
        mob = mob_ref[row : row + 1, :]
        under = mob_lo[...] if row == 0 else mob_ref[row - 1 : row, :]
        over = mob_hi[...] if row == rows - 1 else mob_ref[row + 1 : row + 2, :]
        w_under = 0.04 * (mob + under)
        w_over = 0.04 * (mob + over)
        if row == 0:
            w_under = jnp.where(has_below, w_under, 0.0)
        if row == rows - 1:
            w_over = jnp.where(has_above, w_over, 0.0)
        w_left = jnp.where(column > 0, 0.04 * (mob + pltpu.roll(mob, 1, 1)), 0.0)
        w_right = jnp.where(column < COLS - 1, 0.04 * (mob + pltpu.roll(mob, 127, 1)), 0.0)
        w_plane = 0.04 * (mob + pltpu.roll(mob, COLS, 1))
        own = 1.0 - (w_under + w_over + w_left + w_right + w_plane)
        weight[0, row] = jnp.broadcast_to(w_under, (8, 128))
        weight[1, row] = jnp.broadcast_to(w_over, (8, 128))
        to = lax.broadcasted_iota(jnp.int32, (128, 128), 1)
        gap = to - lax.broadcasted_iota(jnp.int32, (128, 128), 0)
        matrix = jnp.where(gap == 0, own, 0.0)
        matrix = jnp.where(gap == 1, w_left, matrix)
        matrix = jnp.where(gap == -1, w_right, matrix)
        matrix = jnp.where((gap == COLS) | (gap == -COLS), w_plane, matrix)
        main = matrix.astype(jnp.bfloat16)
        rest = (matrix - main.astype(jnp.float32)).astype(jnp.bfloat16)
        across[row, pl.ds(0, 128), pl.ds(0, 128)] = main
        across[row, pl.ds(128, 128), pl.ds(0, 128)] = main
        across[row, pl.ds(0, 128), pl.ds(128, 128)] = rest
        across[row, pl.ds(128, 128), pl.ds(128, 128)] = jnp.zeros((128, 128), jnp.bfloat16)

    lax.fori_loop(0, cuts[1] // JOIN, join_even, 0)
    lax.fori_loop(cuts[2] // JOIN, total_rows // JOIN, join_even, 0)
    even_c = take_sums(0)
    send_late(0, even_c)
    pass_on(1)
    lax.fori_loop(
        first_early // 8, last_early // 8, functools.partial(mix, 0, (0, rows - 1), even_c), 0
    )
    lax.fori_loop(0, ne // 8, functools.partial(mix, 0, middle_rows, even_c), 0)

    wide = min(WIDE, ne)

    def drift(block, carry):
        first = pl.multiple_of(block * wide, wide)
        at = pl.ds(first, wide)
        level = (
            (my_e * ne + first).astype(jnp.float32) + 0.5
            + lax.broadcasted_iota(jnp.int32, (wide, 128), 0).astype(jnp.float32)
        ) * (1.0 / NE)
        drive = 0.25 * (level * lax.rsqrt(level))
        for row in range(rows):
            for field in range(2):
                value = mixed[field, row, at, :]
                main = value.astype(jnp.bfloat16)
                rest = (value - main.astype(jnp.float32)).astype(jnp.bfloat16)
                both = jnp.dot(
                    jnp.concatenate([main, rest], axis=1), across[row],
                    preferred_element_type=jnp.float32,
                )
                result = both[:, :128] + both[:, 128:]
                if row > 0:
                    result = result + weight[0, row, 0:1, :] * mixed[field, row - 1, at, :]
                if row < rows - 1:
                    result = result + weight[1, row, 0:1, :] * mixed[field, row + 1, at, :]
                coupled = drive * mixed[1 - field, row, at, :]
                result = result + coupled if field == 0 else result - coupled
                out[field, pl.ds(first * rows + row, wide, stride=rows), :] = result
        return carry

    lax.fori_loop(0, ne // wide, drift, 0)

    pass_on(0)

    def add_edges(field, step, carry):
        at = pl.multiple_of(step * 8, 8)
        for row, edge_of, side in ((0, lo, 0), (rows - 1, hi, 1)):
            to = pl.ds(at * rows + row, 8, stride=rows)
            out[field, to, :] = (
                out[field, to, :] + weight[side, row] * edge_of[field, pl.ds(at, 8), :]
            )
        return carry

    for copies in early_sends:
        arrive(copies)

    def mix_early(step, carry):
        at = pl.multiple_of(step * 8, 8)
        for side, target in ((0, lo), (1, hi)):
            value = even_c[0] * ahead[side, 0, pl.ds(at, 8), :]
            for term in range(1, HISTORY + 1):
                value = value + even_c[term] * ahead[side, term, pl.ds(at, 8), :]
            target[0, pl.ds(first_early + at, 8), :] = value
        return carry

    lax.fori_loop(0, (last_early - first_early) // 8, mix_early, 0)
    lax.fori_loop(first_early // 8, last_early // 8, functools.partial(add_edges, 0), 0)

    for index, (field, rank, begin, end) in enumerate(late_items):
        arrive(sends[index])
        lax.fori_loop(begin // 8, end // 8, functools.partial(add_edges, field), 0)

    for field in range(2):
        sums_out = gathered.at[field, pl.ds(0, count - 1)]
        pltpu.make_async_copy(sums_out, sums_out, sum_send.at[field]).wait()

    @pl.when(has_above_e)
    def _():
        for up_e, _ in halos:
            up_e.wait_send()

    @pl.when(has_below_e)
    def _():
        for _, down_e in halos:
            down_e.wait_send()

    for index, (field, rank, begin, end) in enumerate(late_items):
        for side, own_kind in ((0, 0), (1, 3)):
            if relayable(field, rank):

                @pl.when(by_relay(field, rank)[side])
                def _():
                    relays[index][side].wait_send()

                @pl.when((kind == own_kind) & (rank < ranks[field][side]))
                def _():
                    onward[index][side].wait_send()

            @pl.when(straight(field, rank)[side])
            def _():
                sends[index][side].wait_send()

    sent = [mobs] + early_sends

    @pl.when(has_above)
    def _():
        for up, _ in sent:
            up.wait_send()

    @pl.when(has_below)
    def _():
        for _, down in sent:
            down.wait_send()


def local(n_egrp, n_space, dist, hist_x, hist_g, mobility, region, phonon_bins, coupling, hist_used):
    ne, rows = dist.shape[1], dist.shape[2]
    total = ne * rows
    pad = KMAX * rows
    count = n_egrp * n_space
    early_plan, late_plan = plan(ne)
    early = early_plan[2] - early_plan[0]
    f32 = jnp.float32
    vmem = pl.BlockSpec(memory_space=pltpu.VMEM)
    hbm = pl.BlockSpec(memory_space=pltpu.HBM)
    result = pl.pallas_call(
        functools.partial(kernel, n_egrp, n_space, ne, rows),
        out_shape=jax.ShapeDtypeStruct((2, total, 128), f32),
        in_specs=[hbm] * 8,
        out_specs=vmem,
        scratch_shapes=[
            pltpu.SMEM((NREGION,), jnp.int32),
            pltpu.SMEM((NREGION,), f32),
            pltpu.SMEM((2, HISTORY), jnp.int32),
            pltpu.VMEM((rows, 128), f32),
            pltpu.VMEM((rows, 128), jnp.int32),
            pltpu.VMEM((total + 2 * pad, 128), f32),
            pltpu.VMEM((total, 128), f32),
            pltpu.VMEM((HISTORY, 2, total, 128), jnp.bfloat16),
            pltpu.VMEM((HISTORY, 2, total, 128), jnp.bfloat16),
            pltpu.VMEM((2, total, 128), f32),
            pltpu.VMEM((total, 128), f32),
            pltpu.VMEM((HISTORY, 2, total, 128), f32),
            pltpu.VMEM((2, rows, ne, 128), f32),
            pltpu.VMEM((2, HISTORY + 1, early, 128), f32),
            pltpu.VMEM((2, ne, 128), f32),
            pltpu.VMEM((2, ne, 128), f32),
            pltpu.VMEM((2, HISTORY + 1, early, 128), f32),
            pltpu.VMEM((6, 8, 128), f32),
            pltpu.VMEM((8, 128), jnp.int32),
            pltpu.VMEM((rows, 256, 256), jnp.bfloat16),
            pltpu.VMEM((2, rows, 8, 128), f32),
            pltpu.VMEM((2, ne, 128), f32),
            pltpu.VMEM((2, 1, 128), f32),
            pltpu.VMEM((1, 128), f32),
            pltpu.VMEM((1, 128), f32),
            pltpu.VMEM((16, 128), f32),
            pltpu.VMEM((2, 1, 128), f32),
            pltpu.VMEM((2, count, 1, 128), f32),
            pltpu.VMEM((2, HALO_PIECES, pad // HALO_PIECES, 128), f32),
            pltpu.SemaphoreType.DMA((10,)),
            pltpu.SemaphoreType.DMA((5,)),
            pltpu.SemaphoreType.DMA((2, HALO_PIECES)),
            pltpu.SemaphoreType.DMA((2, HALO_PIECES)),
            pltpu.SemaphoreType.DMA((2,)),
            pltpu.SemaphoreType.DMA((2,)),
            pltpu.SemaphoreType.DMA((2,)),
            pltpu.SemaphoreType.DMA((2,)),
            pltpu.SemaphoreType.DMA((2, len(late_plan))),
            pltpu.SemaphoreType.DMA((2, len(late_plan))),
            pltpu.SemaphoreType.DMA((2, 3)),
            pltpu.SemaphoreType.DMA((2, 3)),
            pltpu.SemaphoreType.DMA((len(late_plan),)),
            pltpu.SemaphoreType.DMA((len(late_plan),)),
            pltpu.SemaphoreType.DMA((len(late_plan),)),
        ],
        compiler_params=pltpu.CompilerParams(
            collective_id=0, has_side_effects=True, vmem_limit_bytes=40 << 20
        ),
    )(
        *[pltpu.with_memory_space_constraint(x, pltpu.HBM) for x in (phonon_bins, coupling, hist_used, mobility, region,
        dist.reshape(2, total, 128),
        hist_x.reshape(HISTORY, 2, total, 128),
        hist_g.reshape(HISTORY, 2, total, 128))],
    )
    return result.reshape(dist.shape)


def solution(mesh):
    in_specs = (
        P(None, "egrp", "space", None),
        P(None, None, "egrp", "space", None),
        P(None, None, "egrp", "space", None),
        P("space", None),
        P("space", None),
        P(),
        P(),
        P(),
    )
    out_specs = P(None, "egrp", "space", None)
    body = functools.partial(local, mesh.shape["egrp"], mesh.shape["space"])
    return jax.shard_map(body, mesh=mesh, in_specs=in_specs, out_specs=out_specs, check_vma=False)
```
